128 devices in a mesh: grp: 2 (over y_hi), lat: 4 (over z), lon: 16 (over y_lo, x, core).
Axes of the slice: x: 4, y: 4 (y_hi: 2, y_lo: 2; y = y_hi * 2 + y_lo), z: 4, core: 2. Of those that a mesh axis runs over, the one named last changes fastest.
Arguments:
- state: bfloat16 [2, 64, 2048, 512], P('grp', 'lat', 'lon'), may hold values from -6 to 6
- intersection_lists: int32 [2, 4, 16, 3, 64], P('grp', 'lat', 'lon'), may hold values from 0 to 63, as said below
- intersection_matrices: bfloat16 [2, 4, 16, 64, 128, 128], P('grp', 'lat', 'lon'), may hold values from -0.5 to 0.5
- water_indicator: int32 [64, 4096], P('lat', 'lon'), may hold values from 0 to 1, as said below
- atmosphere_kernels: bfloat16 [2, 3, 3, 512, 512], replicated, may hold values from -0.09375 to 0.09375
- ocean_kernels: bfloat16 [2, 3, 3, 256, 256], replicated, may hold values from -0.125 to 0.125
- flux_projection: bfloat16 [512, 256], replicated, may hold values from -0.25 to 0.25
- coupling_matrix: bfloat16 [256, 512], replicated, may hold values from -0.375 to 0.375
Outputs:
- new_state: bfloat16 [2, 64, 2048, 512], P('grp', 'lat', 'lon')
The draws below stay inside these ranges and needn't reach their ends.
Inputs may be any that keep to these rules, and one draw needn't show every extreme that they name: intersection_lists[g, i, j] lists the 64 intersections whose source block lies on tile (i, j) of component g (0 atmosphere, 1 ocean). Row 0 is the tile number of the receiving tile of the other component; row 1 the source block, below 16 for atmosphere sources and below 32 for ocean sources; row 2 the receiving block, below 32 on ocean tiles and below 16 on atmosphere tiles. A source tile names one receiving tile at most 2 times, and every source tile names some receiving tile exactly 2 times. `water_indicator`: the share of land differs from tile to tile.
All inputs are finite; a program needn't handle non-finite values.
Results may differ from the reference program's by a relative error of at most 0.01.
Values may be sent and summed in bfloat16 or wider, within the bound.
A program may use at most 192 MiB of HBM per device.

```python
import jax
import jax.numpy as jnp
from jax import lax

AIR_FEATURES = 512
SEA_FEATURES = 256
PANEL_PARALLELS = 16
PANEL_MERIDIANS = 128
LAYERS = 2
PATCH_PARALLELS = 8
PATCH_MERIDIANS = 16
SLOTS = 2
TILES = 64
ENTRIES = 64
BLOCK = 128
AIR_PATCH_TOTAL = 16
NBO = 32
PARALLEL_LINES = 64
MERIDIAN_TOTAL = 2048
N_LAT = 4
N_LON = 16


def one_list(item_key, group_id, list_index):
    slot_total = TILES * SLOTS
    key_perm, key_owner, key_order, key_source, key_target = jax.random.split(item_key, 5)
    scores = jax.random.permutation(key_perm, slot_total)
    forced = jax.random.randint(key_owner, (), 0, TILES)
    forced = jnp.where(list_index == 0, TILES - 1, forced)
    slot_ids = jnp.arange(slot_total)
    scores = jnp.where(slot_ids // SLOTS == forced, slot_ids % SLOTS - SLOTS, scores)
    picked = jnp.argsort(scores, stable=True)[:ENTRIES]
    picked = picked[jax.random.permutation(key_order, ENTRIES)]
    owners = (picked // SLOTS).astype(jnp.int32)
    source_top = jnp.where(group_id == 0, AIR_PATCH_TOTAL, NBO)
    target_top = jnp.where(group_id == 0, NBO, AIR_PATCH_TOTAL)
    sources = jax.random.randint(key_source, (ENTRIES,), 0, source_top)
    targets = jax.random.randint(key_target, (ENTRIES,), 0, target_top)
    sources = sources.at[0].set(source_top - 1)
    targets = targets.at[0].set(0)
    return jnp.stack([owners, sources.astype(jnp.int32), targets.astype(jnp.int32)])


def draw_intersection_lists(key, part):
    keys = jax.random.split(jax.random.fold_in(key, 11), 2 * TILES)
    group_ids = jnp.repeat(jnp.arange(2), TILES)
    list_ids = jnp.arange(2 * TILES)
    lists = jax.vmap(one_list)(keys, group_ids, list_ids)
    return lists.reshape(2, N_LAT, N_LON, 3, ENTRIES).astype(jnp.int32)


def draw_water_indicator(key, part):
    key_tile, key_cell = jax.random.split(jax.random.fold_in(key, 23))
    land_share = jax.random.randint(key_tile, (N_LAT, 1, N_LON, 1), 0, 80)
    draws = jax.random.randint(key_cell, (N_LAT, PANEL_PARALLELS, N_LON, 2 * PANEL_MERIDIANS), 0, 100)
    return (draws >= land_share).astype(jnp.int32).reshape(PARALLEL_LINES, 2 * MERIDIAN_TOTAL)


def steps_of(stream_key, extent, cuts, smallest, largest):
    def one(dim, blocks):
        heights = jax.random.uniform(jax.random.fold_in(jax.random.fold_in(stream_key, 6), dim), (blocks,), jnp.float32, smallest / len(cuts), largest / len(cuts))
        return jnp.repeat(jnp.exp(heights), extent[dim] // blocks).reshape((-1,) + (1,) * (len(extent) - dim - 1))

    level = one(*cuts[0])
    for cut in cuts[1:]:
        level = level * one(*cut)
    return level


def scatter_about(rng, dims, width, limit, cuts=(), dtype=jnp.bfloat16):
    gain = steps_of(rng, dims, cuts, -0.22, 0.18) if cuts else 1.0
    values = jax.random.normal(rng, dims, jnp.float32) * width * gain
    return jnp.minimum(jnp.maximum(values, -limit), limit).astype(dtype)


def setup_inputs(seed: int = 0) -> dict:
    splits = jax.random.split(jax.random.key(seed), 9)
    return {
        "state": scatter_about(splits[0], (2, PARALLEL_LINES, MERIDIAN_TOTAL, AIR_FEATURES), 1.0, 6.0, ((0, 2), (1, 4), (2, 16))),
        "intersection_lists": draw_intersection_lists(jax.random.fold_in(splits[8], 71), 0),
        "intersection_matrices": scatter_about(splits[2], (2, N_LAT, N_LON, ENTRIES, BLOCK, BLOCK), BLOCK ** -0.5, 0.5, ((0, 2), (1, 4), (2, 16))),
        "water_indicator": draw_water_indicator(jax.random.fold_in(splits[8], 71), 0),
        "atmosphere_kernels": scatter_about(splits[4], (LAYERS, 3, 3, AIR_FEATURES, AIR_FEATURES), (9 * AIR_FEATURES) ** -0.5, 0.09375),
        "ocean_kernels": scatter_about(splits[5], (LAYERS, 3, 3, SEA_FEATURES, SEA_FEATURES), (9 * SEA_FEATURES) ** -0.5, 0.125),
        "flux_projection": scatter_about(splits[6], (AIR_FEATURES, SEA_FEATURES), AIR_FEATURES ** -0.5, 0.25),
        "coupling_matrix": scatter_about(splits[7], (SEA_FEATURES, AIR_FEATURES), SEA_FEATURES ** -0.5, 0.375),
    }


def periodic_conv(hidden, kernel):
    patch_span_down, patch_span_across = hidden.shape[0], hidden.shape[1]
    padded = jnp.pad(hidden, ((1, 1), (0, 0), (0, 0)))
    padded = jnp.concatenate([padded[:, -1:], padded, padded[:, :1]], axis=1)
    patch_totals = jnp.zeros((patch_span_down * patch_span_across, kernel.shape[3]), jnp.float32)
    for shift_row in range(3):
        for shift_col in range(3):
            window = padded[shift_row:shift_row + patch_span_down, shift_col:shift_col + patch_span_across].reshape(patch_span_down * patch_span_across, -1)
            patch_totals = patch_totals + jnp.dot(window, kernel[shift_row, shift_col], preferred_element_type=jnp.float32)
    return patch_totals.reshape(patch_span_down, patch_span_across, -1)


def divide_patches(grid_field, tile_rows, tile_cols):
    patch_span_down, patch_span_across, channels = grid_field.shape
    lat_tiles = patch_span_down // tile_rows
    lon_tiles = patch_span_across // tile_cols
    reshaped = grid_field.reshape(lat_tiles, tile_rows // PATCH_PARALLELS, PATCH_PARALLELS, lon_tiles, tile_cols // PATCH_MERIDIANS, PATCH_MERIDIANS, channels)
    reshaped = reshaped.transpose(0, 3, 1, 4, 2, 5, 6)
    return reshaped.reshape(lat_tiles * lon_tiles, (tile_rows // PATCH_PARALLELS) * (tile_cols // PATCH_MERIDIANS), BLOCK, channels)


def assemble_patches(blocks, tile_rows, tile_cols):
    channels = blocks.shape[-1]
    reshaped = blocks.reshape(N_LAT, N_LON, tile_rows // PATCH_PARALLELS, tile_cols // PATCH_MERIDIANS, PATCH_PARALLELS, PATCH_MERIDIANS, channels)
    reshaped = reshaped.transpose(0, 2, 4, 1, 3, 5, 6)
    return reshaped.reshape(N_LAT * tile_rows, N_LON * tile_cols, channels)


def remap_values(source_blocks, label_lookup, remapping_factors, dest_count):
    def one_tile(patch_totals, entry_item):
        blocks, entry_ids, weight = entry_item
        chosen = blocks[entry_ids[1]]
        payload = jnp.einsum("eij,ejk->eik", weight.astype(jnp.float32), chosen.astype(jnp.float32)).astype(jnp.bfloat16)
        patch_totals = patch_totals.at[entry_ids[0], entry_ids[2]].add(payload.astype(jnp.float32))
        return patch_totals, None

    initial = jnp.zeros((TILES, dest_count, BLOCK, SEA_FEATURES), jnp.float32)
    patch_totals, _ = lax.scan(one_tile, initial, (source_blocks, label_lookup, remapping_factors))
    return patch_totals


def reference(state, intersection_lists, intersection_matrices, water_indicator, atmosphere_kernels, ocean_kernels, flux_projection, coupling_matrix):
    atmos = state[0]
    marine_condition = state[1].reshape(PARALLEL_LINES, 2 * MERIDIAN_TOTAL, SEA_FEATURES)
    flux = jnp.dot(atmos.reshape(-1, AIR_FEATURES), flux_projection, preferred_element_type=jnp.float32).astype(jnp.bfloat16)
    flux = flux.reshape(PARALLEL_LINES, MERIDIAN_TOTAL, SEA_FEATURES)
    skin_warmth = marine_condition * water_indicator.astype(jnp.bfloat16)[:, :, None]
    label_lookup = intersection_lists.reshape(2, TILES, 3, ENTRIES)
    remapping_factors = intersection_matrices.reshape(2, TILES, ENTRIES, BLOCK, BLOCK)
    to_ocean = remap_values(divide_patches(flux, PANEL_PARALLELS, PANEL_MERIDIANS), label_lookup[0], remapping_factors[0], NBO)
    deliver_upward = remap_values(divide_patches(skin_warmth, PANEL_PARALLELS, 2 * PANEL_MERIDIANS), label_lookup[1], remapping_factors[1], AIR_PATCH_TOTAL)
    ocean_force = assemble_patches(to_ocean, PANEL_PARALLELS, 2 * PANEL_MERIDIANS)
    skin_warmth_given = assemble_patches(deliver_upward, PANEL_PARALLELS, PANEL_MERIDIANS).astype(jnp.bfloat16)
    air_driving_term = jnp.dot(skin_warmth_given.reshape(-1, SEA_FEATURES), coupling_matrix, preferred_element_type=jnp.float32).reshape(PARALLEL_LINES, MERIDIAN_TOTAL, AIR_FEATURES)
    ocean_mask = water_indicator.astype(jnp.float32)[:, :, None]
    for layer_index in range(LAYERS):
        hidden = jax.nn.silu(atmos.astype(jnp.float32)).astype(jnp.bfloat16)
        update = atmos.astype(jnp.float32) + periodic_conv(hidden, atmosphere_kernels[layer_index])
        if layer_index == 0:
            update = update + air_driving_term
        atmos = update.astype(jnp.bfloat16)
        hidden = jax.nn.silu(marine_condition.astype(jnp.float32)).astype(jnp.bfloat16)
        update = marine_condition.astype(jnp.float32) + periodic_conv(hidden, ocean_kernels[layer_index])
        if layer_index == 0:
            update = update + ocean_force
        marine_condition = (update * ocean_mask).astype(jnp.bfloat16)
    return jnp.stack([atmos, marine_condition.reshape(PARALLEL_LINES, MERIDIAN_TOTAL, AIR_FEATURES)])
```

```python
from functools import partial

import jax
import jax.numpy as jnp
from jax import lax
from jax.experimental import pallas as pl
from jax.experimental.pallas import tpu as pltpu
from jax.sharding import PartitionSpec as P

LAYERS = 2
ROWS = 16
COLS = 128
WIDE = 512
HALF = 256
BLOCK = 128
ENTRIES = 64
TILES = 64
CHUNKS = 4
PIECE = BLOCK // CHUNKS
SLOT_TOTAL = 2 * TILES
MESH = pl.DeviceIdType.MESH
F32 = jnp.float32
BF16 = jnp.bfloat16


def dot(a, b):
    return jnp.dot(a, b, preferred_element_type=F32)


def place_entries(lists, counts, places, labels_ref):
    def clear(i, _):
        counts[i] = 0
        labels_ref[0, 2 * i] = -1
        labels_ref[0, 2 * i + 1] = -1
        return 0

    lax.fori_loop(0, TILES, clear, 0)

    def place(e, _):
        owner = lists[0, e]
        rank = counts[owner]
        counts[owner] = rank + 1
        slot = 2 * (owner ^ 8) + rank
        places[e] = slot
        labels_ref[0, slot] = lists[2, e]
        return 0

    lax.fori_loop(0, ENTRIES, place, 0)


def write_payloads(lists, places, factors, blocks, out_ref):
    def one(e, _):
        value = dot(factors[e], blocks[lists[1, e]])
        out_ref[0, places[e]] = value.astype(BF16)
        return 0

    lax.fori_loop(0, ENTRIES, one, 0, unroll=8)


def air_payloads(lists, state, factors, projection, out_ref, labels_ref, blocks, counts, places):
    @pl.when(pl.program_id(0) == 0)
    def _():
        place_entries(lists, counts, places, labels_ref)
        for row in range(ROWS):
            flux = dot(state[row], projection[...]).astype(BF16)
            band, sub = row // 8, row % 8
            blocks[8 * band : 8 * band + 8, 16 * sub : 16 * sub + 16, :] = flux.reshape(8, 16, HALF)

    write_payloads(lists, places, factors, blocks, out_ref)


def interleave_matrix():
    cell = lax.broadcasted_iota(jnp.int32, (BLOCK, BLOCK), 0)
    place = lax.broadcasted_iota(jnp.int32, (BLOCK, BLOCK), 1)
    wanted = (cell % 2) * 64 + (cell // 16) * 8 + (cell % 16) // 2
    return (wanted == place).astype(F32).astype(BF16)


def sea_payloads(lists, state, factors, water, out_ref, labels_ref, halves, blocks, counts, places):
    @pl.when(pl.program_id(0) == 0)
    def _():
        place_entries(lists, counts, places, labels_ref)
        for row in range(ROWS):
            band, sub = row // 8, row % 8
            for side in range(2):
                surface = state[row, :, side * HALF : (side + 1) * HALF].astype(F32)
                surface = surface * water[row, :, side : side + 1]
                start = 64 * side + 8 * sub
                halves[16 * band : 16 * band + 16, start : start + 8, :] = surface.reshape(16, 8, HALF)
        order = interleave_matrix()

        def one(b, _):
            blocks[b] = dot(order, halves[b].astype(BF16)).astype(BF16)
            return 0

        lax.fori_loop(0, 32, one, 0, unroll=4)

    write_payloads(lists, places, factors, blocks, out_ref)


def payload_call(kernel, block_total, extra, lists, state, factors, side):
    whole = lambda shape: pl.BlockSpec(shape, lambda c, *_: (0,) * len(shape))
    return pl.pallas_call(
        kernel,
        out_shape=(
            jax.ShapeDtypeStruct((CHUNKS, SLOT_TOTAL, PIECE, HALF), BF16),
            jax.ShapeDtypeStruct((1, SLOT_TOTAL), jnp.int32),
        ),
        grid_spec=pltpu.PrefetchScalarGridSpec(
            num_scalar_prefetch=1,
            grid=(CHUNKS,),
            in_specs=[
                whole(state.shape),
                pl.BlockSpec((ENTRIES, PIECE, BLOCK), lambda c, *_: (0, c, 0)),
                whole(side.shape),
            ],
            out_specs=(
                pl.BlockSpec((1, SLOT_TOTAL, PIECE, HALF), lambda c, *_: (c, 0, 0, 0)),
                pl.BlockSpec(memory_space=pltpu.SMEM),
            ),
            scratch_shapes=extra
            + [
                pltpu.VMEM((block_total, BLOCK, HALF), BF16),
                pltpu.SMEM((TILES,), jnp.int32),
                pltpu.SMEM((ENTRIES,), jnp.int32),
            ],
        ),
        compiler_params=pltpu.CompilerParams(vmem_limit_bytes=40 << 20),
    )(lists, state, factors, side)


def sort_slots(labels_ref, me, orders):
    labels = labels_ref[...].reshape(TILES, SLOT_TOTAL)
    lane = lax.broadcasted_iota(jnp.int32, (TILES, SLOT_TOTAL), 1)
    first = jnp.sum(jnp.where(lane == 2 * me, labels, 0), axis=1, keepdims=True)
    second = jnp.sum(jnp.where(lane == 2 * me + 1, labels, 0), axis=1, keepdims=True)
    column = jnp.concatenate([first, second], axis=0)
    down = lax.broadcasted_iota(jnp.int32, (SLOT_TOTAL, SLOT_TOTAL), 0)
    across = lax.broadcasted_iota(jnp.int32, (SLOT_TOTAL, SLOT_TOTAL), 1)
    keys = jnp.broadcast_to(column, (SLOT_TOTAL, SLOT_TOTAL))
    row = jnp.sum(jnp.where(down == across, keys, 0), axis=0, keepdims=True)
    other = jnp.broadcast_to(row, (SLOT_TOTAL, SLOT_TOTAL))
    ahead = (other < keys) | ((other == keys) & (across < down))
    rank = jnp.sum(ahead.astype(jnp.int32), axis=1, keepdims=True)
    hit = rank == across
    slot = 2 * (down % TILES) + down // TILES
    order = jnp.sum(jnp.where(hit, slot, 0), axis=0, keepdims=True)
    sorted_keys = jnp.sum(jnp.where(hit, keys, 0), axis=0, keepdims=True)
    previous = jnp.sum(jnp.where(rank + 1 == across, keys, 0), axis=0, keepdims=True)
    lanes = lax.broadcasted_iota(jnp.int32, (1, SLOT_TOTAL), 1)
    opens = ((sorted_keys != previous) | (lanes == 0)).astype(jnp.int32)
    count = jnp.sum((keys == across).astype(jnp.int32), axis=0, keepdims=True)
    last = jnp.sum((keys <= across).astype(jnp.int32), axis=0, keepdims=True) - 1
    last = jnp.maximum(last, 0)
    orders[...] = jnp.concatenate([order, opens, last, count, order, opens, last, count], axis=0)


def exchange(payload, labels, out_ref, recv_0, recv_1, recv_2, recv_3, marks, orders, table, sums, leaving, arriving, sent, landed, own, mark_sem, local_sem, over_sent, over_landed):
    recv = [recv_0, recv_1, recv_2, recv_3]
    grp, lat, lon = lax.axis_index("grp"), lax.axis_index("lat"), lax.axis_index("lon")
    me = lat * 16 + lon
    high, x, core = lon // 8, (lon // 2) % 4, lon % 2
    facing = (1 - grp, lat, (lon + 8) % 16)

    def target(k):
        z = (lat + k) % 4
        y = (high + k // 16 + k // 2) % 2
        c = (core + k // 32 + k) % 2
        return z, y * 8 + ((x + k // 4 + k) % 4) * 2 + c

    barrier = pltpu.get_barrier_semaphore()

    def greet(k, _):
        z, j = target(k)
        pl.semaphore_signal(barrier, inc=1, device_id=(grp, z, j), device_id_type=MESH)
        return 0

    lax.fori_loop(1, TILES, greet, 0)
    pl.semaphore_signal(barrier, inc=1, device_id=facing, device_id_type=MESH)
    pl.semaphore_wait(barrier, TILES)

    def send_label(k, _):
        z, j = target(k)
        pltpu.make_async_remote_copy(
            labels, marks.at[me], mark_sem.at[0], mark_sem.at[1], device_id=(grp, z, j), device_id_type=MESH
        ).start()
        return 0

    lax.fori_loop(1, TILES, send_label, 0)
    mine = pltpu.make_async_copy(labels, marks.at[me], local_sem.at[0])
    mine.start()

    for chunk in range(CHUNKS):

        def send(k, _):
            z, j = target(k)
            pltpu.make_async_remote_copy(
                payload.at[chunk, pl.ds(2 * (z * 16 + j), 2)],
                recv[chunk].at[pl.ds(2 * me, 2)],
                sent.at[chunk],
                landed.at[chunk],
                device_id=(grp, z, j),
                device_id_type=MESH,
            ).start()
            return 0

        lax.fori_loop(1, TILES, send, 0)
        pltpu.make_async_copy(
            payload.at[chunk, pl.ds(2 * me, 2)], recv[chunk].at[pl.ds(2 * me, 2)], own.at[chunk]
        ).start()

    mine.wait()
    others = pltpu.make_async_remote_copy(
        marks.at[pl.ds(0, TILES - 1)],
        marks.at[pl.ds(0, TILES - 1)],
        mark_sem.at[0],
        mark_sem.at[1],
        device_id=facing,
        device_id_type=MESH,
    )
    others.wait_recv()
    others.wait_send()
    sort_slots(marks, me, orders)
    move = pltpu.make_async_copy(orders, table, local_sem.at[1])
    move.start()
    move.wait()

    def crossing(chunk, part):
        blocks = pl.ds(16 * part, 16)
        return pltpu.make_async_remote_copy(
            leaving.at[chunk, blocks],
            arriving.at[chunk, blocks],
            over_sent.at[chunk, part],
            over_landed.at[chunk, part],
            device_id=facing,
            device_id_type=MESH,
        )

    for chunk in range(CHUNKS):
        pltpu.make_async_copy(
            payload.at[chunk, pl.ds(2 * me, 2)], recv[chunk].at[pl.ds(2 * me, 2)], own.at[chunk]
        ).wait()
        rest = pltpu.make_async_remote_copy(
            payload.at[chunk, pl.ds(0, SLOT_TOTAL - 2)],
            recv[chunk].at[pl.ds(0, SLOT_TOTAL - 2)],
            sent.at[chunk],
            landed.at[chunk],
            device_id=facing,
            device_id_type=MESH,
        )
        rest.wait_recv()
        rest.wait_send()

        def accumulate(p, total):
            value = recv[chunk][table[0, p]].astype(F32)
            total = jnp.where(table[1, p] == 1, 0.0, total) + value
            sums[p] = total
            return total

        lax.fori_loop(0, SLOT_TOTAL, accumulate, jnp.zeros((PIECE, HALF), F32), unroll=8)

        def settle(b, _):
            value = jnp.where(table[3, b] > 0, sums[table[2, b]], 0.0)
            leaving[chunk, b] = value.astype(BF16)
            return 0

        lax.fori_loop(0, 32, settle, 0, unroll=4)
        crossing(chunk, 0).start()

        @pl.when(grp == 0)
        def _():
            crossing(chunk, 1).start()

    for chunk in range(CHUNKS):
        crossing(chunk, 0).wait()

        @pl.when(grp == 0)
        def _():
            crossing(chunk, 1).wait_send()

        @pl.when(grp == 1)
        def _():
            crossing(chunk, 1).wait_recv()

    out = pltpu.make_async_copy(arriving.at[:, pl.ds(0, 16)], out_ref.at[:, pl.ds(0, 16)], local_sem.at[2])
    out.start()

    @pl.when(grp == 1)
    def _():
        rest = pltpu.make_async_copy(
            arriving.at[:, pl.ds(16, 16)], out_ref.at[:, pl.ds(16, 16)], local_sem.at[3]
        )
        rest.start()
        rest.wait()

    out.wait()


def exchange_call(payload, labels):
    dma = pltpu.SemaphoreType.DMA
    return pl.pallas_call(
        exchange,
        out_shape=jax.ShapeDtypeStruct((CHUNKS, 32, PIECE, HALF), BF16),
        in_specs=[pl.BlockSpec(memory_space=pl.ANY), pl.BlockSpec(memory_space=pltpu.VMEM)],
        out_specs=pl.BlockSpec(memory_space=pl.ANY),
        scratch_shapes=[pltpu.VMEM((SLOT_TOTAL, PIECE, HALF), BF16)] * CHUNKS
        + [
            pltpu.VMEM((TILES, 1, SLOT_TOTAL), jnp.int32),
            pltpu.VMEM((8, SLOT_TOTAL), jnp.int32),
            pltpu.SMEM((8, SLOT_TOTAL), jnp.int32),
            pltpu.VMEM((SLOT_TOTAL, PIECE, HALF), F32),
            pltpu.VMEM((CHUNKS, 32, PIECE, HALF), BF16),
            pltpu.VMEM((CHUNKS, 32, PIECE, HALF), BF16),
            dma((CHUNKS,)),
            dma((CHUNKS,)),
            dma((CHUNKS,)),
            dma((2,)),
            dma((4,)),
            dma((CHUNKS, 2)),
            dma((CHUNKS, 2)),
        ],
        compiler_params=pltpu.CompilerParams(
            collective_id=0, has_side_effects=True, vmem_limit_bytes=48 << 20
        ),
    )(payload, labels)


def silu(value):
    return value / (1.0 + jnp.exp(-value))


def rows_with_rims(sides, rims, lat):
    above = rims[0].astype(F32)[15:16] * jnp.where(lat == 0, 0.0, 1.0)
    below = rims[2].astype(F32)[0:1] * jnp.where(lat == 3, 0.0, 1.0)
    sides[0:1, :] = above
    sides[1:17, :] = rims[1].astype(F32)
    sides[17:18, :] = below


def layer_kernel(layer, forced, state, force, coupling, water, air_kernels, sea_kernels, out_ref, padded, edges, rims, sides, ends, air, sea, fetch, sent, landed):
    grp, lat, lon = lax.axis_index("grp"), lax.axis_index("lat"), lax.axis_index("lon")
    west, east = (lon + 15) % 16, (lon + 1) % 16
    north, south = (lat + 3) % 4, (lat + 1) % 4

    get_air = pltpu.make_async_copy(air_kernels.at[layer], air, fetch)
    get_sea = pltpu.make_async_copy(sea_kernels.at[layer], sea, fetch)

    @pl.when(grp == 0)
    def _():
        get_air.start()

    @pl.when(grp == 1)
    def _():
        get_sea.start()

    barrier = pltpu.get_barrier_semaphore()
    near = [(north, lon), (south, lon)] + [(z, j) for j in (west, east) for z in (north, lat, south)]
    for z, j in near:
        pl.semaphore_signal(barrier, inc=1, device_id=(grp, z, j), device_id_type=MESH)

    def activate(row, _):
        padded[row + 1] = silu(state[row].astype(F32)).astype(BF16)
        return 0

    lax.fori_loop(0, ROWS, activate, 0, unroll=2)
    for side, first in ((0, 0), (1, COLS - 16)):
        group = padded[1:17, first : first + 16, :].astype(F32)
        edges[side] = group[:, 15 * side, :].astype(BF16)

    pl.semaphore_wait(barrier, 8)

    def push(index, source, target, z, j):
        copy = pltpu.make_async_remote_copy(
            source, target, sent.at[index], landed.at[index], device_id=(grp, z, j), device_id_type=MESH
        )
        copy.start()
        return copy

    copies = [
        push(0, padded.at[1], padded.at[17], north, lon),
        push(1, padded.at[16], padded.at[0], south, lon),
    ]
    for side, j in ((0, west), (1, east)):
        for index, z, place in ((0, north, 2), (1, lat, 1), (2, south, 0)):
            copies.append(push(2 + 3 * side + index, edges.at[side], rims.at[1 - side, place], z, j))
    for copy in copies:
        copy.wait()

    @pl.when(lat == 0)
    def _():
        padded[0] = jnp.zeros((COLS, WIDE), BF16)

    @pl.when(lat == 3)
    def _():
        padded[17] = jnp.zeros((COLS, WIDE), BF16)

    for side in range(2):
        rows_with_rims(sides.at[side], rims.at[side], lat)
    column = lax.broadcasted_iota(jnp.int32, (COLS, 1), 0)

    def moved(value, edge, shift):
        rolled = pltpu.roll(value, shift % COLS, 0)
        return jnp.where(column == (0 if shift == 1 else COLS - 1), edge, rolled)

    @pl.when(grp == 0)
    def _():
        get_air.wait()
        for side, tap in ((0, 0), (1, 2)):
            ends[side] = sum(dot(sides[side, r : r + 16, :].astype(BF16), air[r, tap]) for r in range(3))

        def some_rows(step, _):
            first = 4 * step
            parts = []
            for tap in range(3):
                total = None
                for r in range(3):
                    window = padded[pl.ds(first + r, 4)].reshape(4 * COLS, WIDE)
                    term = dot(window, air[r, tap])
                    total = term if total is None else total + term
                parts.append(total)
            for i in range(4):
                row = first + i
                low = slice(i * COLS, (i + 1) * COLS)
                value = state[row].astype(F32) + parts[1][low]
                value = value + moved(parts[0][low], ends[0, pl.ds(row, 1), :], 1)
                value = value + moved(parts[2][low], ends[1, pl.ds(row, 1), :], -1)
                if forced:
                    given = force[i // 2 + 2 * (step % 2), pl.ds(8 * (step // 2), 8), 16 * (i % 2) : 16 * (i % 2) + 16, :]
                    value = value + dot(given.reshape(COLS, HALF), coupling[...])
                out_ref[row] = value.astype(BF16)
            return 0

        lax.fori_loop(0, 4, some_rows, 0)

    @pl.when(grp == 1)
    def _():
        get_sea.wait()
        ends[0, :, 0:HALF] = sum(dot(sides[0, r : r + 16, HALF:].astype(BF16), sea[r, 0]) for r in range(3))
        ends[1, :, 0:HALF] = sum(dot(sides[1, r : r + 16, :HALF].astype(BF16), sea[r, 2]) for r in range(3))
        cell = lax.broadcasted_iota(jnp.int32, (COLS, 2 * COLS), 1)
        pair = lax.broadcasted_iota(jnp.int32, (COLS, 2 * COLS), 0)

        def some_rows(step, _):
            first = 4 * step
            low = high = from_west = from_east = None
            for r in range(3):
                window = padded[pl.ds(first + r, 4)].reshape(4 * COLS, WIDE)
                even, odd = window[:, :HALF], window[:, HALF:]
                terms = (
                    dot(even, sea[r, 1]) + dot(odd, sea[r, 2]),
                    dot(even, sea[r, 0]) + dot(odd, sea[r, 1]),
                    dot(odd, sea[r, 0]),
                    dot(even, sea[r, 2]),
                )
                if low is None:
                    low, high, from_west, from_east = terms
                else:
                    low, high = low + terms[0], high + terms[1]
                    from_west, from_east = from_west + terms[2], from_east + terms[3]
            for i in range(4):
                row = first + i
                part = slice(i * COLS, (i + 1) * COLS)
                old = state[row].astype(F32)
                sides_now = [
                    low[part] + moved(from_west[part], ends[0, pl.ds(row, 1), 0:HALF], 1),
                    high[part] + moved(from_east[part], ends[1, pl.ds(row, 1), 0:HALF], -1),
                ]
                for side in range(2):
                    lanes = slice(side * HALF, (side + 1) * HALF)
                    value = old[:, lanes] + sides_now[side]
                    if forced:
                        given = force[i // 2 + 2 * (step % 2), pl.ds(16 * (step // 2), 16), 16 * (i % 2) : 16 * (i % 2) + 16, :]
                        pick = (cell == 2 * pair + side).astype(F32).astype(BF16)
                        value = value + dot(pick, given.reshape(2 * COLS, HALF))
                    out_ref[row, :, lanes] = (value * water[row, :, side : side + 1]).astype(BF16)
            return 0

        lax.fori_loop(0, 4, some_rows, 0)


def layer_call(layer, forced, state, force, coupling, water, air_kernels, sea_kernels):
    dma = pltpu.SemaphoreType.DMA
    vmem = pl.BlockSpec(memory_space=pltpu.VMEM)
    hbm = pl.BlockSpec(memory_space=pl.ANY)
    return pl.pallas_call(
        partial(layer_kernel, layer, forced),
        out_shape=jax.ShapeDtypeStruct((ROWS, COLS, WIDE), BF16),
        in_specs=[vmem, vmem, vmem, vmem, hbm, hbm],
        out_specs=vmem,
        scratch_shapes=[
            pltpu.VMEM((ROWS + 2, COLS, WIDE), BF16),
            pltpu.VMEM((2, 16, WIDE), BF16),
            pltpu.VMEM((2, 3, 16, WIDE), BF16),
            pltpu.VMEM((2, 24, WIDE), F32),
            pltpu.VMEM((2, 16, WIDE), F32),
            pltpu.VMEM((3, 3, WIDE, WIDE), BF16),
            pltpu.VMEM((3, 3, HALF, HALF), BF16),
            dma,
            dma((8,)),
            dma((8,)),
        ],
        compiler_params=pltpu.CompilerParams(
            collective_id=1 + layer, has_side_effects=True, vmem_limit_bytes=56 << 20
        ),
    )(state, force, coupling, water, air_kernels, sea_kernels)


def body(
    state,
    intersection_lists,
    intersection_matrices,
    water_indicator,
    atmosphere_kernels,
    ocean_kernels,
    flux_projection,
    coupling_matrix,
):
    current = state[0]
    lists = intersection_lists.reshape(3, ENTRIES)
    factors = intersection_matrices.reshape(ENTRIES, BLOCK, BLOCK)
    water = water_indicator.astype(F32).reshape(ROWS, COLS, 2)

    def sea(_):
        halves = [pltpu.VMEM((32, BLOCK, HALF), F32)]
        return payload_call(sea_payloads, 32, halves, lists, current, factors, water)

    def air(_):
        return payload_call(air_payloads, 16, [], lists, current, factors, flux_projection)

    payload, labels = lax.cond(lax.axis_index("grp") == 1, sea, air, 0)
    force = exchange_call(payload, labels)
    for layer in range(LAYERS):
        current = layer_call(
            layer, layer == 0, current, force, coupling_matrix, water, atmosphere_kernels, ocean_kernels
        )
    return current[None]


def solution(mesh):
    placed = (
        P("grp", "lat", "lon", None),
        P("grp", "lat", "lon", None, None),
        P("grp", "lat", "lon", None, None, None),
        P("lat", "lon"),
        P(),
        P(),
        P(),
        P(),
    )
    return jax.shard_map(
        body, mesh=mesh, in_specs=placed, out_specs=P("grp", "lat", "lon", None), check_vma=False
    )
```

```python
import jax
import jax.numpy as jnp
from jax import lax
from jax.experimental import pallas as pl
from jax.experimental.pallas import tpu as pltpu
from jax.sharding import PartitionSpec as P

ROWS = 16
COLS = 128
WIDE = 512
HALF = 256
BLOCK = 128
ENTRIES = 64
TILES = 64
SLOT_TOTAL = 2 * TILES
CHUNKS = ((0, 2), (2, 2), (4, 2), (6, 1), (7, 1))
EARLY_CHUNKS = 3
PIECES = tuple(16 * count for _, count in CHUNKS)
N = len(CHUNKS)
MESH = pl.DeviceIdType.MESH
F32 = jnp.float32
BF16 = jnp.bfloat16


def dot(a, b):
    return jnp.dot(a, b, preferred_element_type=F32)


def iota(shape, dim):
    return lax.broadcasted_iota(jnp.int32, shape, dim)


def ones_where(condition):
    return condition.astype(F32).astype(BF16)


def silu(value):
    return value / (1.0 + jnp.exp(-value))


def activated(value):
    return silu(value.astype(F32)).astype(BF16)


def place_entries(lists, labels, places):
    down, across = iota((ENTRIES, ENTRIES), 0), iota((ENTRIES, ENTRIES), 1)

    def column(row):
        return jnp.sum(jnp.where(down == across, row, 0), axis=1, keepdims=True)

    owner_row = lists[0:1, :]
    owner, source, target = column(owner_row), column(lists[1:2, :]), column(lists[2:3, :])
    rank = jnp.sum(((owner_row == owner) & (across < down)).astype(jnp.int32), axis=1, keepdims=True)
    slot = 2 * jnp.bitwise_xor(owner, 8) + rank
    hit = slot == iota((ENTRIES, SLOT_TOTAL), 1)
    entry = jnp.sum(jnp.where(hit, iota((ENTRIES, SLOT_TOTAL), 0), 0), axis=0, keepdims=True)
    taken = jnp.sum(jnp.where(hit, source, 0), axis=0, keepdims=True)
    labels[...] = jnp.sum(jnp.where(hit, target + 1, 0), axis=0, keepdims=True) - 1
    places[...] = jnp.concatenate([entry, taken] * 4, axis=0)


def sort_slots(labels_ref, me, orders):
    labels = labels_ref[...].reshape(TILES, SLOT_TOTAL)
    lane = iota((TILES, SLOT_TOTAL), 1)
    first = jnp.sum(jnp.where(lane == 2 * me, labels, 0), axis=1, keepdims=True)
    second = jnp.sum(jnp.where(lane == 2 * me + 1, labels, 0), axis=1, keepdims=True)
    column = jnp.concatenate([first, second], axis=0)
    down, across = iota((SLOT_TOTAL, SLOT_TOTAL), 0), iota((SLOT_TOTAL, SLOT_TOTAL), 1)
    keys = jnp.broadcast_to(column, (SLOT_TOTAL, SLOT_TOTAL))
    row = jnp.sum(jnp.where(down == across, keys, 0), axis=0, keepdims=True)
    other = jnp.broadcast_to(row, (SLOT_TOTAL, SLOT_TOTAL))
    ahead = (other < keys) | ((other == keys) & (across < down))
    rank = jnp.sum(ahead.astype(jnp.int32), axis=1, keepdims=True)
    hit = rank == across
    slot = 2 * (down % TILES) + down // TILES
    order = jnp.sum(jnp.where(hit, slot, 0), axis=0, keepdims=True)
    sorted_keys = jnp.sum(jnp.where(hit, keys, 0), axis=0, keepdims=True)
    previous = jnp.sum(jnp.where(rank + 1 == across, keys, 0), axis=0, keepdims=True)
    opens = ((sorted_keys != previous) | (iota((1, SLOT_TOTAL), 1) == 0)).astype(jnp.int32)
    count = jnp.sum((keys == across).astype(jnp.int32), axis=0, keepdims=True)
    last = jnp.sum((keys <= across).astype(jnp.int32), axis=0, keepdims=True) - 1
    last = jnp.maximum(last, 0)
    orders[...] = jnp.concatenate([order, opens, last, count] * 2, axis=0)


def air_blocks(state, projection, blocks):
    for row in range(ROWS):
        flux = dot(state[row], projection[...]).astype(BF16)
        band, sub = row // 8, row % 8
        blocks[8 * band : 8 * band + 8, 16 * sub : 16 * sub + 16, :] = flux.reshape(8, 16, HALF)


def sea_blocks(state, water, mask, halves, blocks):
    cell, pair = iota((COLS, 2 * COLS), 1), iota((COLS, 2 * COLS), 0)
    ones = jnp.ones((2 * COLS, HALF), F32).astype(BF16)
    for row in range(ROWS):
        band, sub = row // 8, row % 8
        for side in range(2):
            wet = jnp.where(cell == 2 * pair + side, water[row : row + 1, :], 0).astype(F32).astype(BF16)
            wet = dot(wet, ones)
            lanes = slice(side * HALF, (side + 1) * HALF)
            mask[row, :, lanes] = wet.astype(BF16)
            surface = (state[row, :, lanes].astype(F32) * wet).reshape(16, 8, HALF)
            start = 64 * side + 8 * sub
            for b in range(16):
                halves[4 * (16 * band + b) + start // 32, start % 32 : start % 32 + 8, :] = surface[b]
    cell, place = iota((BLOCK, BLOCK), 0), iota((BLOCK, BLOCK), 1)
    order = ones_where((cell % 2) * 64 + (cell // 16) * 8 + (cell % 16) // 2 == place)

    def one(b, _):
        blocks[b] = dot(order, halves[pl.ds(4 * b, 4)].reshape(BLOCK, HALF).astype(BF16)).astype(BF16)
        return 0

    lax.fori_loop(0, 32, one, 0, unroll=4)


def moved_east(value):
    return jnp.where(iota((COLS, 1), 0) == 0, 0.0, pltpu.roll(value, 1, 0))


def moved_west(value):
    return jnp.where(iota((COLS, 1), 0) == COLS - 1, 0.0, pltpu.roll(value, COLS - 1, 0))


def total(terms):
    result = terms[0]
    for term in terms[1:]:
        result = result + term
    return result


def mix_air(windows, kernel):
    west, here, east = (total([dot(windows[r], kernel[r, tap]) for r in range(3)]) for tap in range(3))
    rows = [slice(i * COLS, (i + 1) * COLS) for i in range(here.shape[0] // COLS)]
    return [here[row] + moved_east(west[row]) + moved_west(east[row]) for row in rows]


def mix_sea(windows, kernel):
    even = [window[:, :HALF] for window in windows]
    odd = [window[:, HALF:] for window in windows]
    low = total([dot(even[r], kernel[r, 1]) + dot(odd[r], kernel[r, 2]) for r in range(3)])
    high = total([dot(even[r], kernel[r, 0]) + dot(odd[r], kernel[r, 1]) for r in range(3)])
    west = total([dot(odd[r], kernel[r, 0]) for r in range(3)])
    east = total([dot(even[r], kernel[r, 2]) for r in range(3)])
    rows = [slice(i * COLS, (i + 1) * COLS) for i in range(low.shape[0] // COLS)]
    return [
        jnp.concatenate([low[row] + moved_east(west[row]), high[row] + moved_west(east[row])], axis=1)
        for row in rows
    ]


def step_kernel(
    lists, state_in, factors_in, water, air_in, sea_in, projection_in, coupling_in, out_ref, *scratch
):
    send, scratch = scratch[:N], scratch[N:]
    recv, scratch = scratch[:N], scratch[N:]
    leaving, scratch = scratch[:N], scratch[N:]
    arriving, scratch = scratch[:N], scratch[N:]
    (state, factors, projection, coupling, air, sea, blocks, mask, sums, acc) = scratch[:10]
    (padded_0, padded_1, edges_0, edges_1, rims_0, rims_1, sides, ends, saved) = scratch[10:19]
    (labels, marks, places, place_table, orders, order_table) = scratch[19:25]
    (fetch, local_sem, own, sent, landed, mark_sem, over_sent, over_landed, rim_sent, rim_landed) = scratch[25:]

    grp, lat, lon = lax.axis_index("grp"), lax.axis_index("lat"), lax.axis_index("lon")
    me = lat * 16 + lon
    high, x, core = lon // 8, (lon // 2) % 4, lon % 2
    facing = (1 - grp, lat, (lon + 8) % 16)
    west, east = (lon + 15) % 16, (lon + 1) % 16
    north, south = (lat + 3) % 4, (lat + 1) % 4

    def target(k):
        z = (lat + k) % 4
        y = (high + k // 16 + k // 2) % 2
        c = (core + k // 32 + k) % 2
        return z, y * 8 + ((x + k // 4 + k) % 4) * 2 + c

    get_state = pltpu.make_async_copy(state_in, state, fetch.at[0])
    get_factors = pltpu.make_async_copy(factors_in, factors, fetch.at[1])
    get_projection = pltpu.make_async_copy(projection_in, projection, fetch.at[2])
    get_coupling = pltpu.make_async_copy(coupling_in, coupling, fetch.at[3])
    get_air = [pltpu.make_async_copy(air_in.at[layer], air, fetch.at[4 + layer]) for layer in range(2)]
    get_sea = [pltpu.make_async_copy(sea_in.at[layer], sea, fetch.at[4 + layer]) for layer in range(2)]
    get_state.start()
    get_projection.start()
    get_factors.start()
    get_coupling.start()

    def on_air(body):
        pl.when(grp == 0)(body)

    def on_sea(body):
        pl.when(grp == 1)(body)

    on_air(get_air[0].start)
    on_sea(get_sea[0].start)

    barrier = pltpu.get_barrier_semaphore()

    def greet(k, _):
        z, j = target(k)
        pl.semaphore_signal(barrier, inc=1, device_id=(grp, z, j), device_id_type=MESH)
        return 0

    lax.fori_loop(1, TILES, greet, 0)
    pl.semaphore_signal(barrier, inc=1, device_id=facing, device_id_type=MESH)

    place_entries(lists, labels, places)
    tell = pltpu.make_async_copy(places, place_table, local_sem.at[0])
    tell.start()

    get_state.wait()
    padded_0[1] = activated(state[0])
    padded_0[16] = activated(state[ROWS - 1])
    for side, first in ((0, 0), (1, COLS - 16)):
        group = silu(state[:, first : first + 16, :].astype(F32))
        edges_0[side] = group[:, 15 * side, :].astype(BF16)

    def rim_copies(layer, padded, edges, rims):
        pushes = [(padded.at[1], padded.at[17], north, lon), (padded.at[16], padded.at[0], south, lon)]
        for side, j in ((0, west), (1, east)):
            for z, place in ((north, 2), (lat, 1), (south, 0)):
                pushes.append((edges.at[side], rims.at[1 - side, place], z, j))
        return [
            pltpu.make_async_remote_copy(
                source,
                goal,
                rim_sent.at[layer, index],
                rim_landed.at[layer, index],
                device_id=(grp, z, j),
                device_id_type=MESH,
            )
            for index, (source, goal, z, j) in enumerate(pushes)
        ]

    first_rims = rim_copies(0, padded_0, edges_0, rims_0)
    pl.semaphore_wait(barrier, TILES)
    for copy in first_rims:
        copy.start()

    def send_label(k, _):
        z, j = target(k)
        pltpu.make_async_remote_copy(
            labels, marks.at[me], mark_sem.at[0], mark_sem.at[1], device_id=(grp, z, j), device_id_type=MESH
        ).start()
        return 0

    lax.fori_loop(1, TILES, send_label, 0)
    own_label = pltpu.make_async_copy(labels, marks.at[me], local_sem.at[1])
    own_label.start()

    @on_air
    def _():
        get_projection.wait()
        air_blocks(state, projection, blocks)

    @on_sea
    def _():
        get_projection.wait()
        sea_blocks(state, water, mask, sums, blocks)

    get_factors.wait()
    tell.wait()

    def write_payloads(chunks):
        start = 16 * CHUNKS[chunks[0]][0]
        length = sum(PIECES[chunk] for chunk in chunks)

        def one(slot, _):
            factor = factors[place_table[0, slot], start : start + length, :]
            value = dot(factor, blocks[place_table[1, slot]]).astype(BF16)
            offset = 0
            for chunk in chunks:
                send[chunk][slot] = value[offset : offset + PIECES[chunk]]
                offset += PIECES[chunk]
            return 0

        lax.fori_loop(0, SLOT_TOTAL, one, 0, unroll=8)

    def own_copy(chunk):
        mine = pl.ds(2 * me, 2)
        return pltpu.make_async_copy(send[chunk].at[mine], recv[chunk].at[mine], own.at[chunk])

    def send_payloads(chunk):
        def one(k, _):
            z, j = target(k)
            pltpu.make_async_remote_copy(
                send[chunk].at[pl.ds(2 * (z * 16 + j), 2)],
                recv[chunk].at[pl.ds(2 * me, 2)],
                sent.at[chunk],
                landed.at[chunk],
                device_id=(grp, z, j),
                device_id_type=MESH,
            ).start()
            return 0

        lax.fori_loop(1, TILES, one, 0)
        own_copy(chunk).start()

    write_payloads((0,))
    send_payloads(0)
    write_payloads(tuple(range(1, N)))
    for chunk in range(1, N):
        send_payloads(chunk)

    def activate(row, _):
        padded_0[row + 1] = activated(state[row])
        return 0

    lax.fori_loop(1, ROWS - 1, activate, 0, unroll=2)
    for copy in first_rims:
        copy.wait()

    def close_rims(padded, rims):
        @pl.when(lat == 0)
        def _():
            padded[0] = jnp.zeros((COLS, WIDE), BF16)

        @pl.when(lat == 3)
        def _():
            padded[17] = jnp.zeros((COLS, WIDE), BF16)

        for side in range(2):
            sides[side, 0:1, :] = rims[side, 0].astype(F32)[15:16] * jnp.where(lat == 0, 0.0, 1.0)
            sides[side, 1:17, :] = rims[side, 1].astype(F32)
            sides[side, 17:18, :] = rims[side, 2].astype(F32)[0:1] * jnp.where(lat == 3, 0.0, 1.0)

    def end_columns():
        @on_air
        def _():
            for side, tap in ((0, 0), (1, 2)):
                ends[side] = total([dot(sides[side, r : r + 16, :].astype(BF16), air[r, tap]) for r in range(3)])

        @on_sea
        def _():
            nothing = jnp.zeros((ROWS, HALF), F32)
            first = total([dot(sides[0, r : r + 16, HALF:].astype(BF16), sea[r, 0]) for r in range(3)])
            final = total([dot(sides[1, r : r + 16, :HALF].astype(BF16), sea[r, 2]) for r in range(3)])
            ends[0] = jnp.concatenate([first, nothing], axis=1)
            ends[1] = jnp.concatenate([nothing, final], axis=1)

    def mixed_rows(mix, kernel):
        def some_rows(step, _):
            windows = [padded_0[pl.ds(4 * step + r, 4)].reshape(4 * COLS, WIDE) for r in range(3)]
            for i, value in enumerate(mix(windows, kernel)):
                acc[4 * step + i] = value + state[4 * step + i].astype(F32)
            return 0

        lax.fori_loop(0, 4, some_rows, 0)

    close_rims(padded_0, rims_0)

    @on_air
    def _():
        get_air[0].wait()
        mixed_rows(mix_air, air)

    @on_sea
    def _():
        get_sea[0].wait()
        mixed_rows(mix_sea, sea)

    end_columns()
    eight = iota((8, 1), 0)

    def add_ends(row, _):
        acc[row, 0:8, :] += jnp.where(eight == 0, ends[0, pl.ds(row, 1), :], 0.0)
        acc[row, COLS - 8 : COLS, :] += jnp.where(eight == 7, ends[1, pl.ds(row, 1), :], 0.0)
        return 0

    lax.fori_loop(0, ROWS, add_ends, 0)
    on_air(get_air[1].start)
    on_sea(get_sea[1].start)
    get_coupling.wait()

    own_label.wait()
    others = pltpu.make_async_remote_copy(
        marks.at[pl.ds(0, TILES - 1)],
        marks.at[pl.ds(0, TILES - 1)],
        mark_sem.at[0],
        mark_sem.at[1],
        device_id=facing,
        device_id_type=MESH,
    )
    others.wait_recv()
    others.wait_send()
    sort_slots(marks, me, orders)
    tell_order = pltpu.make_async_copy(orders, order_table, local_sem.at[2])
    tell_order.start()
    tell_order.wait()

    def crossing(chunk, part):
        half = pl.ds(16 * part, 16)
        return pltpu.make_async_remote_copy(
            leaving[chunk].at[half],
            arriving[chunk].at[half],
            over_sent.at[chunk, part],
            over_landed.at[chunk, part],
            device_id=facing,
            device_id_type=MESH,
        )

    def sum_and_cross(chunk):
        piece = PIECES[chunk]
        own_copy(chunk).wait()
        rest = pl.ds(0, SLOT_TOTAL - 2)
        everyone = pltpu.make_async_remote_copy(
            send[chunk].at[rest],
            recv[chunk].at[rest],
            sent.at[chunk],
            landed.at[chunk],
            device_id=facing,
            device_id_type=MESH,
        )
        everyone.wait_recv()
        everyone.wait_send()

        def accumulate(p, running):
            value = recv[chunk][order_table[0, p]].astype(F32)
            running = jnp.where(order_table[1, p] == 1, 0.0, running) + value
            sums[p, 0:piece, :] = running
            return running

        lax.fori_loop(0, SLOT_TOTAL, accumulate, jnp.zeros((piece, HALF), F32), unroll=8)

        def settle(b, _):
            value = jnp.where(order_table[3, b] > 0, sums[order_table[2, b], 0:piece, :], 0.0)
            leaving[chunk][b] = value.astype(BF16)
            return 0

        lax.fori_loop(0, 32, settle, 0, unroll=4)
        crossing(chunk, 0).start()
        on_air(crossing(chunk, 1).start)

    def finish_rows(chunk):
        crossing(chunk, 0).wait()
        on_air(crossing(chunk, 1).wait_send)
        on_sea(crossing(chunk, 1).wait_recv)
        first, count = CHUNKS[chunk]
        wanted = [(band, i, 8 * band + first + i) for band in range(2) for i in range(count)]

        @on_air
        def _():
            for band, i, row in wanted:
                given = arriving[chunk][8 * band : 8 * band + 8, 16 * i : 16 * i + 16, :]
                value = (acc[row] + dot(given.reshape(COLS, HALF), coupling[...])).astype(BF16)
                state[row] = value
                padded_1[row + 1] = activated(value)

        @on_sea
        def _():
            cell, pair = iota((COLS, 2 * COLS), 1), iota((COLS, 2 * COLS), 0)
            for band, i, row in wanted:
                given = arriving[chunk][16 * band : 16 * band + 16, 16 * i : 16 * i + 16, :]
                given = given.reshape(2 * COLS, HALF)
                parts = [dot(ones_where(cell == 2 * pair + side), given) for side in range(2)]
                value = (acc[row] + jnp.concatenate(parts, axis=1)) * mask[row].astype(F32)
                value = value.astype(BF16)
                state[row] = value
                padded_1[row + 1] = activated(value)

    def last_rows(rows):
        def windows():
            return [jnp.concatenate([padded_1[row + r] for row in rows], axis=0) for r in range(3)]

        @on_air
        def _():
            for row, value in zip(rows, mix_air(windows(), air)):
                value = value + state[row].astype(F32)
                saved[0, row] = value[0:16]
                saved[1, row] = value[COLS - 16 : COLS]
                out_ref[row] = value.astype(BF16)

        @on_sea
        def _():
            for row, value in zip(rows, mix_sea(windows(), sea)):
                value = value + state[row].astype(F32)
                saved[0, row] = value[0:16]
                saved[1, row] = value[COLS - 16 : COLS]
                out_ref[row] = (value * mask[row].astype(F32)).astype(BF16)

    for chunk in range(N):
        sum_and_cross(chunk)
        if 1 <= chunk <= EARLY_CHUNKS:
            finish_rows(chunk - 1)
    on_air(get_air[1].wait)
    on_sea(get_sea[1].wait)
    last_rows((1, 2, 3, 4))
    finish_rows(EARLY_CHUNKS)
    last_rows((9, 10, 11, 12))
    for chunk in range(EARLY_CHUNKS + 1, N):
        finish_rows(chunk)

    for side, first in ((0, 0), (1, COLS - 16)):
        group = padded_1[1:17, first : first + 16, :].astype(F32)
        edges_1[side] = group[:, 15 * side, :].astype(BF16)
    last_rims = rim_copies(1, padded_1, edges_1, rims_1)
    for copy in last_rims:
        copy.start()
    last_rows((5, 6, 7, 8))
    last_rows((13, 14))
    for copy in last_rims:
        copy.wait()
    close_rims(padded_1, rims_1)
    last_rows((0, 15))
    end_columns()
    sixteen = iota((16, 1), 0)

    def patch(row, _):
        left = saved[0, row] + jnp.where(sixteen == 0, ends[0, pl.ds(row, 1), :], 0.0)
        right = saved[1, row] + jnp.where(sixteen == 15, ends[1, pl.ds(row, 1), :], 0.0)

        @on_air
        def _():
            out_ref[row, 0:16, :] = left.astype(BF16)
            out_ref[row, COLS - 16 : COLS, :] = right.astype(BF16)

        @on_sea
        def _():
            out_ref[row, 0:16, :] = (left * mask[row, 0:16, :].astype(F32)).astype(BF16)
            out_ref[row, COLS - 16 : COLS, :] = (right * mask[row, COLS - 16 : COLS, :].astype(F32)).astype(BF16)

        return 0

    lax.fori_loop(0, ROWS, patch, 0)


def body(
    state,
    intersection_lists,
    intersection_matrices,
    water_indicator,
    atmosphere_kernels,
    ocean_kernels,
    flux_projection,
    coupling_matrix,
):
    dma = pltpu.SemaphoreType.DMA
    vmem = pl.BlockSpec(memory_space=pltpu.VMEM)
    hbm = pl.BlockSpec(memory_space=pl.ANY)
    tables = pltpu.VMEM((8, SLOT_TOTAL), jnp.int32)
    scalars = pltpu.SMEM((8, SLOT_TOTAL), jnp.int32)
    slots = [pltpu.VMEM((SLOT_TOTAL, piece, HALF), BF16) for piece in PIECES]
    dense = [pltpu.VMEM((32, piece, HALF), BF16) for piece in PIECES]
    result = pl.pallas_call(
        step_kernel,
        out_shape=jax.ShapeDtypeStruct((ROWS, COLS, WIDE), BF16),
        in_specs=[vmem, hbm, hbm, vmem, hbm, hbm, hbm, hbm],
        out_specs=vmem,
        scratch_shapes=slots
        + slots
        + dense
        + dense
        + [
            pltpu.VMEM((ROWS, COLS, WIDE), BF16),
            pltpu.VMEM((ENTRIES, BLOCK, BLOCK), BF16),
            pltpu.VMEM((WIDE, HALF), BF16),
            pltpu.VMEM((HALF, WIDE), BF16),
            pltpu.VMEM((3, 3, WIDE, WIDE), BF16),
            pltpu.VMEM((3, 3, HALF, HALF), BF16),
            pltpu.VMEM((32, BLOCK, HALF), BF16),
            pltpu.VMEM((ROWS, COLS, WIDE), BF16),
            pltpu.VMEM((SLOT_TOTAL, 32, HALF), F32),
            pltpu.VMEM((ROWS, COLS, WIDE), F32),
            pltpu.VMEM((ROWS + 2, COLS, WIDE), BF16),
            pltpu.VMEM((ROWS + 2, COLS, WIDE), BF16),
            pltpu.VMEM((2, 16, WIDE), BF16),
            pltpu.VMEM((2, 16, WIDE), BF16),
            pltpu.VMEM((2, 3, 16, WIDE), BF16),
            pltpu.VMEM((2, 3, 16, WIDE), BF16),
            pltpu.VMEM((2, 24, WIDE), F32),
            pltpu.VMEM((2, 16, WIDE), F32),
            pltpu.VMEM((2, ROWS, 16, WIDE), F32),
            pltpu.VMEM((1, SLOT_TOTAL), jnp.int32),
            pltpu.VMEM((TILES, 1, SLOT_TOTAL), jnp.int32),
            tables,
            scalars,
            tables,
            scalars,
            dma((6,)),
            dma((3,)),
            dma((N,)),
            dma((N,)),
            dma((N,)),
            dma((2,)),
            dma((N, 2)),
            dma((N, 2)),
            dma((2, 8)),
            dma((2, 8)),
        ],
        compiler_params=pltpu.CompilerParams(
            collective_id=0, has_side_effects=True, vmem_limit_bytes=63 << 20
        ),
    )(
        intersection_lists.reshape(3, ENTRIES),
        state[0],
        intersection_matrices.reshape(ENTRIES, BLOCK, BLOCK),
        water_indicator,
        atmosphere_kernels,
        ocean_kernels,
        flux_projection,
        coupling_matrix,
    )
    return result[None]


def solution(mesh):
    placed = (
        P("grp", "lat", "lon", None),
        P("grp", "lat", "lon", None, None),
        P("grp", "lat", "lon", None, None, None),
        P("lat", "lon"),
        P(),
        P(),
        P(),
        P(),
    )
    return jax.shard_map(
        body, mesh=mesh, in_specs=placed, out_specs=P("grp", "lat", "lon", None), check_vma=False
    )
```

```python
import jax
import jax.numpy as jnp
from jax import lax
from jax.experimental import pallas as pl
from jax.experimental.pallas import tpu as pltpu
from jax.sharding import PartitionSpec as P

ROWS = 16
COLS = 128
WIDE = 512
HALF = 256
BLOCK = 128
ENTRIES = 64
TILES = 64
SLOT_TOTAL = 2 * TILES
CHUNKS = ((0, 2, 0, 256), (2, 2, 0, 256), (4, 2, 0, 256), (6, 1, 0, 256), (7, 1, 0, 128), (7, 1, 128, 128))
PIECES = tuple((16 * chunk[1], chunk[3]) for chunk in CHUNKS)
N = len(CHUNKS)
MESH = pl.DeviceIdType.MESH
F32 = jnp.float32
BF16 = jnp.bfloat16


def dot(a, b):
    return jnp.dot(a, b, preferred_element_type=F32)


def iota(shape, dim):
    return lax.broadcasted_iota(jnp.int32, shape, dim)


def ones_where(condition):
    return condition.astype(F32).astype(BF16)


def silu(value):
    return value / (1.0 + jnp.exp(-value))


def activated(value):
    return silu(value.astype(F32)).astype(BF16)


def place_entries(lists, labels, places):
    down, across = iota((ENTRIES, ENTRIES), 0), iota((ENTRIES, ENTRIES), 1)

    def column(row):
        return jnp.sum(jnp.where(down == across, row, 0), axis=1, keepdims=True)

    owner_row = lists[0]
    owner, source, target = column(owner_row), column(lists[1]), column(lists[2])
    rank = jnp.sum(((owner_row == owner) & (across < down)).astype(jnp.int32), axis=1, keepdims=True)
    slot = 2 * jnp.bitwise_xor(owner, 8) + rank
    hit = slot == iota((ENTRIES, SLOT_TOTAL), 1)
    entry = jnp.sum(jnp.where(hit, iota((ENTRIES, SLOT_TOTAL), 0), 0), axis=0, keepdims=True)
    taken = jnp.sum(jnp.where(hit, source, 0), axis=0, keepdims=True)
    labels[...] = jnp.sum(jnp.where(hit, target + 1, 0), axis=0, keepdims=True) - 1
    places[...] = jnp.concatenate([entry, taken] * 4, axis=0)


def sort_slots(labels_ref, me, orders):
    labels = labels_ref[...].reshape(TILES, SLOT_TOTAL)
    lane = iota((TILES, SLOT_TOTAL), 1)
    first = jnp.sum(jnp.where(lane == 2 * me, labels, 0), axis=1, keepdims=True)
    second = jnp.sum(jnp.where(lane == 2 * me + 1, labels, 0), axis=1, keepdims=True)
    column = jnp.concatenate([first, second], axis=0)
    down, across = iota((SLOT_TOTAL, SLOT_TOTAL), 0), iota((SLOT_TOTAL, SLOT_TOTAL), 1)
    keys = jnp.broadcast_to(column, (SLOT_TOTAL, SLOT_TOTAL))
    row = jnp.sum(jnp.where(down == across, keys, 0), axis=0, keepdims=True)
    other = jnp.broadcast_to(row, (SLOT_TOTAL, SLOT_TOTAL))
    ahead = (other < keys) | ((other == keys) & (across < down))
    rank = jnp.sum(ahead.astype(jnp.int32), axis=1, keepdims=True)
    hit = rank == across
    slot = 2 * (down % TILES) + down // TILES
    order = jnp.sum(jnp.where(hit, slot, 0), axis=0, keepdims=True)
    sorted_keys = jnp.sum(jnp.where(hit, keys, 0), axis=0, keepdims=True)
    previous = jnp.sum(jnp.where(rank + 1 == across, keys, 0), axis=0, keepdims=True)
    opens = ((sorted_keys != previous) | (iota((1, SLOT_TOTAL), 1) == 0)).astype(jnp.int32)
    count = jnp.sum((keys == across).astype(jnp.int32), axis=0, keepdims=True)
    last = jnp.sum((keys <= across).astype(jnp.int32), axis=0, keepdims=True) - 1
    last = jnp.maximum(last, 0)
    orders[...] = jnp.concatenate([order, opens, last, count] * 2, axis=0)


def air_blocks(state, projection, blocks):
    for row in range(ROWS):
        flux = dot(state[row], projection[...]).astype(BF16)
        band, sub = row // 8, row % 8
        blocks[8 * band : 8 * band + 8, 16 * sub : 16 * sub + 16, :] = flux.reshape(8, 16, HALF)


def sea_blocks(state, water, mask, halves, blocks):
    cell, pair = iota((COLS, 2 * COLS), 1), iota((COLS, 2 * COLS), 0)
    ones = jnp.ones((2 * COLS, HALF), F32).astype(BF16)
    for row in range(ROWS):
        band, sub = row // 8, row % 8
        for side in range(2):
            wet = jnp.where(cell == 2 * pair + side, water[row : row + 1, :], 0).astype(F32).astype(BF16)
            wet = dot(wet, ones)
            lanes = slice(side * HALF, (side + 1) * HALF)
            mask[row, :, lanes] = wet.astype(BF16)
            surface = (state[row, :, lanes].astype(F32) * wet).reshape(16, 8, HALF)
            start = 64 * side + 8 * sub
            for b in range(16):
                halves[4 * (16 * band + b) + start // 32, start % 32 : start % 32 + 8, :] = surface[b]
    cell, place = iota((BLOCK, BLOCK), 0), iota((BLOCK, BLOCK), 1)
    order = ones_where((cell % 2) * 64 + (cell // 16) * 8 + (cell % 16) // 2 == place)

    def one(b, _):
        blocks[b] = dot(order, halves[pl.ds(4 * b, 4)].reshape(BLOCK, HALF).astype(BF16)).astype(BF16)
        return 0

    lax.fori_loop(0, 32, one, 0, unroll=4)


def moved_east(value):
    return jnp.where(iota((COLS, 1), 0) == 0, 0.0, pltpu.roll(value, 1, 0))


def moved_west(value):
    return jnp.where(iota((COLS, 1), 0) == COLS - 1, 0.0, pltpu.roll(value, COLS - 1, 0))


def total(terms):
    result = terms[0]
    for term in terms[1:]:
        result = result + term
    return result


def row_parts(value):
    return [value[i * COLS : (i + 1) * COLS] for i in range(value.shape[0] // COLS)]


def mix_air(windows, kernel, sides=None):
    left = right = windows
    if sides is not None:
        left, right = ([jnp.concatenate(pair, axis=0) for pair in zip(windows, side)] for side in sides)
    west = total([dot(left[r], kernel[r, 0]) for r in range(3)])
    here = total([dot(windows[r], kernel[r, 1]) for r in range(3)])
    east = total([dot(right[r], kernel[r, 2]) for r in range(3)])
    rows = [a + moved_east(b) + moved_west(c) for a, b, c in zip(*map(row_parts, (here, west, east)))]
    if sides is None:
        return rows
    size = here.shape[0]
    return rows, (west[size:], east[size:])


def mix_sea(windows, kernel, sides=None):
    even = [window[:, :HALF] for window in windows]
    odd = [window[:, HALF:] for window in windows]
    left, right = odd, even
    if sides is not None:
        left = [jnp.concatenate([a, b[:, HALF:]], axis=0) for a, b in zip(odd, sides[0])]
        right = [jnp.concatenate([a, b[:, :HALF]], axis=0) for a, b in zip(even, sides[1])]
    low = total([dot(even[r], kernel[r, 1]) + dot(odd[r], kernel[r, 2]) for r in range(3)])
    high = total([dot(even[r], kernel[r, 0]) + dot(odd[r], kernel[r, 1]) for r in range(3)])
    west = total([dot(left[r], kernel[r, 0]) for r in range(3)])
    east = total([dot(right[r], kernel[r, 2]) for r in range(3)])
    rows = [
        jnp.concatenate([a + moved_east(c), b + moved_west(d)], axis=1)
        for a, b, c, d in zip(*map(row_parts, (low, high, west, east)))
    ]
    if sides is None:
        return rows
    size = low.shape[0]
    nothing = jnp.zeros((ROWS, HALF), F32)
    ends = jnp.concatenate([west[size:], nothing], axis=1), jnp.concatenate([nothing, east[size:]], axis=1)
    return rows, ends


def step_kernel(
    lists, state_in, factors_in, water, air_in, sea_in, projection_in, coupling_in, out_ref, *scratch
):
    send, scratch = scratch[:N], scratch[N:]
    recv, scratch = scratch[:N], scratch[N:]
    leaving, scratch = scratch[:N], scratch[N:]
    arriving, scratch = scratch[:N], scratch[N:]
    (state, factors, projection, coupling, air, sea, blocks, mask, sums, acc) = scratch[:10]
    (padded_0, padded_1, edges_0, edges_1, rims_0, rims_1, sides, ends, saved) = scratch[10:19]
    (labels, marks, places, place_table, orders, order_table) = scratch[19:25]
    (fetch, local_sem, own, sent, landed, mark_sem, over_sent, over_landed, rim_sent, rim_landed) = scratch[25:]

    grp, lat, lon = lax.axis_index("grp"), lax.axis_index("lat"), lax.axis_index("lon")
    me = lat * 16 + lon
    high, x, core = lon // 8, (lon // 2) % 4, lon % 2
    facing = (1 - grp, lat, (lon + 8) % 16)
    west, east = (lon + 15) % 16, (lon + 1) % 16
    north, south = (lat + 3) % 4, (lat + 1) % 4

    def target(k):
        z = (lat + k) % 4
        y = (high + k // 16 + k // 2) % 2
        c = (core + k // 32 + k) % 2
        return z, y * 8 + ((x + k // 4 + k) % 4) * 2 + c

    get_state = pltpu.make_async_copy(state_in, state, fetch.at[0])
    get_factors = pltpu.make_async_copy(factors_in, factors, fetch.at[1])
    get_projection = pltpu.make_async_copy(projection_in, projection, fetch.at[2])
    get_coupling = pltpu.make_async_copy(coupling_in, coupling, fetch.at[3])
    get_air = [pltpu.make_async_copy(air_in.at[layer], air, fetch.at[4 + layer]) for layer in range(2)]
    get_sea = [pltpu.make_async_copy(sea_in.at[layer], sea, fetch.at[4 + layer]) for layer in range(2)]
    get_state.start()
    get_projection.start()
    get_factors.start()
    get_coupling.start()

    def on_air(body):
        pl.when(grp == 0)(body)

    def on_sea(body):
        pl.when(grp == 1)(body)

    on_air(get_air[0].start)
    on_sea(get_sea[0].start)

    barrier = pltpu.get_barrier_semaphore()

    def greet(k, _):
        z, j = target(k)
        pl.semaphore_signal(barrier, inc=1, device_id=(grp, z, j), device_id_type=MESH)
        return 0

    lax.fori_loop(1, TILES, greet, 0)
    pl.semaphore_signal(barrier, inc=1, device_id=facing, device_id_type=MESH)

    place_entries(lists, labels, places)
    tell = pltpu.make_async_copy(places, place_table, local_sem.at[0])
    tell.start()

    def rim_copies(layer, padded, edges, rims):
        pushes = [(padded.at[1], padded.at[17], north, lon), (padded.at[16], padded.at[0], south, lon)]
        for side, j in ((0, west), (1, east)):
            for z, place in ((north, 2), (lat, 1), (south, 0)):
                pushes.append((edges.at[side], rims.at[1 - side, place], z, j))
        return [
            pltpu.make_async_remote_copy(
                source,
                goal,
                rim_sent.at[layer, index],
                rim_landed.at[layer, index],
                device_id=(grp, z, j),
                device_id_type=MESH,
            )
            for index, (source, goal, z, j) in enumerate(pushes)
        ]

    get_state.wait()

    @on_air
    def _():
        get_projection.wait()
        air_blocks(state, projection, blocks)

    @on_sea
    def _():
        get_projection.wait()
        sea_blocks(state, water, mask, sums, blocks)

    get_factors.wait()
    tell.wait()

    def payload(slot, start, length):
        factor = factors[place_table[0, slot], start : start + length, :]
        return dot(factor, blocks[place_table[1, slot]]).astype(BF16)

    def own_copy(chunk):
        mine = pl.ds(2 * me, 2)
        return pltpu.make_async_copy(send[chunk].at[mine], recv[chunk].at[mine], own.at[chunk])

    def start_send(chunk, k):
        z, j = target(k)
        pltpu.make_async_remote_copy(
            send[chunk].at[pl.ds(2 * (z * 16 + j), 2)],
            recv[chunk].at[pl.ds(2 * me, 2)],
            sent.at[chunk],
            landed.at[chunk],
            device_id=(grp, z, j),
            device_id_type=MESH,
        ).start()

    def send_payloads(chunk):
        def one(k, _):
            start_send(chunk, k)
            return 0

        lax.fori_loop(1, TILES, one, 0)
        own_copy(chunk).start()

    def first_payloads(k):
        z, j = target(k)
        for i in range(2):
            slot = 2 * (z * 16 + j) + i
            send[0][slot] = payload(slot, 0, PIECES[0][0])

    def first_step(k, _):
        first_payloads(k)
        start_send(0, k - 1)
        return 0

    pl.semaphore_wait(barrier, TILES)
    first_payloads(0)
    first_payloads(1)
    lax.fori_loop(2, TILES, first_step, 0, unroll=2)
    start_send(0, TILES - 1)
    own_copy(0).start()

    padded_0[1] = activated(state[0])
    padded_0[16] = activated(state[ROWS - 1])
    for side, first in ((0, 0), (1, COLS - 16)):
        group = silu(state[:, first : first + 16, :].astype(F32))
        edges_0[side] = group[:, 15 * side, :].astype(BF16)
    first_rims = rim_copies(0, padded_0, edges_0, rims_0)

    def send_label(k, _):
        z, j = target(k)
        pltpu.make_async_remote_copy(
            labels, marks.at[me], mark_sem.at[0], mark_sem.at[1], device_id=(grp, z, j), device_id_type=MESH
        ).start()
        return 0

    lax.fori_loop(1, TILES, send_label, 0)
    own_label = pltpu.make_async_copy(labels, marks.at[me], local_sem.at[1])
    own_label.start()

    for copy in first_rims:
        copy.start()

    later = 16 * CHUNKS[1][0]

    def later_payloads(slot, _):
        value = payload(slot, later, BLOCK - later)
        for chunk in range(1, N):
            first, count, lane, lanes = CHUNKS[chunk]
            start = 16 * first - later
            send[chunk][slot] = value[start : start + 16 * count, lane : lane + lanes]
        return 0

    lax.fori_loop(0, SLOT_TOTAL, later_payloads, 0, unroll=8)
    for chunk in range(1, N):
        send_payloads(chunk)

    def activate(row, _):
        padded_0[row + 1] = activated(state[row])
        return 0

    lax.fori_loop(1, ROWS - 1, activate, 0, unroll=2)
    for copy in first_rims:
        copy.wait()

    def close_rims(padded, rims):
        @pl.when(lat == 0)
        def _():
            padded[0] = jnp.zeros((COLS, WIDE), BF16)

        @pl.when(lat == 3)
        def _():
            padded[17] = jnp.zeros((COLS, WIDE), BF16)

        for side in range(2):
            sides[side, 0:1, :] = rims[side, 0].astype(F32)[15:16] * jnp.where(lat == 0, 0.0, 1.0)
            sides[side, 1:17, :] = rims[side, 1].astype(F32)
            sides[side, 17:18, :] = rims[side, 2].astype(F32)[0:1] * jnp.where(lat == 3, 0.0, 1.0)

    def end_columns():
        @on_air
        def _():
            for side, tap in ((0, 0), (1, 2)):
                ends[side] = total([dot(sides[side, r : r + 16, :].astype(BF16), air[r, tap]) for r in range(3)])

        @on_sea
        def _():
            nothing = jnp.zeros((ROWS, HALF), F32)
            first = total([dot(sides[0, r : r + 16, HALF:].astype(BF16), sea[r, 0]) for r in range(3)])
            final = total([dot(sides[1, r : r + 16, :HALF].astype(BF16), sea[r, 2]) for r in range(3)])
            ends[0] = jnp.concatenate([first, nothing], axis=1)
            ends[1] = jnp.concatenate([nothing, final], axis=1)

    def mixed_rows(mix, kernel):
        def some_rows(step, _):
            windows = [padded_0[pl.ds(4 * step + r, 4)].reshape(4 * COLS, WIDE) for r in range(3)]
            for i, value in enumerate(mix(windows, kernel)):
                acc[4 * step + i] = value + state[4 * step + i].astype(F32)
            return 0

        lax.fori_loop(0, 4, some_rows, 0)

    close_rims(padded_0, rims_0)

    @on_air
    def _():
        get_air[0].wait()
        mixed_rows(mix_air, air)

    @on_sea
    def _():
        get_sea[0].wait()
        mixed_rows(mix_sea, sea)

    end_columns()
    eight = iota((8, 1), 0)

    def add_ends(row, _):
        acc[row, 0:8, :] += jnp.where(eight == 0, ends[0, pl.ds(row, 1), :], 0.0)
        acc[row, COLS - 8 : COLS, :] += jnp.where(eight == 7, ends[1, pl.ds(row, 1), :], 0.0)
        return 0

    lax.fori_loop(0, ROWS, add_ends, 0)
    on_air(get_air[1].start)
    on_sea(get_sea[1].start)
    get_coupling.wait()

    own_label.wait()
    others = pltpu.make_async_remote_copy(
        marks.at[pl.ds(0, TILES - 1)],
        marks.at[pl.ds(0, TILES - 1)],
        mark_sem.at[0],
        mark_sem.at[1],
        device_id=facing,
        device_id_type=MESH,
    )
    others.wait_recv()
    others.wait_send()
    sort_slots(marks, me, orders)
    tell_order = pltpu.make_async_copy(orders, order_table, local_sem.at[2])
    tell_order.start()
    tell_order.wait()

    def crossing(chunk, part):
        half = pl.ds(16 * part, 16)
        return pltpu.make_async_remote_copy(
            leaving[chunk].at[half],
            arriving[chunk].at[half],
            over_sent.at[chunk, part],
            over_landed.at[chunk, part],
            device_id=facing,
            device_id_type=MESH,
        )

    def sum_and_cross(chunk):
        piece, lanes = PIECES[chunk]
        own_copy(chunk).wait()
        rest = pl.ds(0, SLOT_TOTAL - 2)
        everyone = pltpu.make_async_remote_copy(
            send[chunk].at[rest],
            recv[chunk].at[rest],
            sent.at[chunk],
            landed.at[chunk],
            device_id=facing,
            device_id_type=MESH,
        )
        everyone.wait_recv()
        everyone.wait_send()

        def accumulate(p, running):
            value = recv[chunk][order_table[0, p]].astype(F32)
            running = jnp.where(order_table[1, p] == 1, 0.0, running) + value
            sums[p, 0:piece, 0:lanes] = running
            return running

        lax.fori_loop(0, SLOT_TOTAL, accumulate, jnp.zeros((piece, lanes), F32), unroll=8)

        def settle(b, _):
            value = jnp.where(order_table[3, b] > 0, sums[order_table[2, b], 0:piece, 0:lanes], 0.0)
            leaving[chunk][b] = value.astype(BF16)
            return 0

        lax.fori_loop(0, 32, settle, 0, unroll=4)
        crossing(chunk, 0).start()
        on_air(crossing(chunk, 1).start)

    def finish_rows(*chunks):
        for chunk in chunks:
            crossing(chunk, 0).wait()
            on_air(crossing(chunk, 1).wait_send)
            on_sea(crossing(chunk, 1).wait_recv)
        first, count = CHUNKS[chunks[0]][:2]
        wanted = [(band, i, 8 * band + first + i) for band in (1, 0) for i in range(count)]

        def given(band, i, blocks_across):
            here = slice(blocks_across * band, blocks_across * (band + 1))
            parts = [arriving[chunk][here, 16 * i : 16 * i + 16, :] for chunk in chunks]
            parts = [part.reshape(16 * blocks_across, part.shape[2]) for part in parts]
            return parts[0] if len(parts) == 1 else jnp.concatenate(parts, axis=1)

        @on_air
        def _():
            for band, i, row in wanted:
                value = (acc[row] + dot(given(band, i, 8), coupling[...])).astype(BF16)
                state[row] = value
                padded_1[row + 1] = activated(value)

        @on_sea
        def _():
            cell, pair = iota((COLS, 2 * COLS), 1), iota((COLS, 2 * COLS), 0)
            for band, i, row in wanted:
                force = given(band, i, 16)
                parts = [dot(ones_where(cell == 2 * pair + side), force) for side in range(2)]
                value = (acc[row] + jnp.concatenate(parts, axis=1)) * mask[row].astype(F32)
                value = value.astype(BF16)
                state[row] = value
                padded_1[row + 1] = activated(value)

    def last_rows(rows, closing=False):
        def windows():
            return [jnp.concatenate([padded_1[row + r] for row in rows], axis=0) for r in range(3)]

        def mixed(mix, kernel):
            if not closing:
                return mix(windows(), kernel)
            rims = [[sides[side, r : r + 16, :].astype(BF16) for r in range(3)] for side in range(2)]
            values, (first, final) = mix(windows(), kernel, rims)
            ends[0] = first
            ends[1] = final
            return values

        def put(row, value, wet):
            value = value + state[row].astype(F32)
            saved[0, row] = value[0:16]
            saved[1, row] = value[COLS - 16 : COLS]
            out_ref[row] = (value if wet is None else value * wet).astype(BF16)

        @on_air
        def _():
            for row, value in zip(rows, mixed(mix_air, air)):
                put(row, value, None)

        @on_sea
        def _():
            for row, value in zip(rows, mixed(mix_sea, sea)):
                put(row, value, mask[row].astype(F32))

    last_rims = rim_copies(1, padded_1, edges_1, rims_1)
    sum_and_cross(0)
    sum_and_cross(1)
    finish_rows(0)
    last_rims[0].start()
    sum_and_cross(2)
    finish_rows(1)
    sum_and_cross(3)
    finish_rows(2)
    on_air(get_air[1].wait)
    on_sea(get_sea[1].wait)
    last_rows((1, 2, 3, 4))
    last_rows((9, 10, 11, 12))
    finish_rows(3)
    sum_and_cross(4)
    last_rows((5, 13))
    sum_and_cross(5)
    finish_rows(4, 5)
    last_rims[1].start()
    for side, first in ((0, 0), (1, COLS - 16)):
        group = padded_1[1:17, first : first + 16, :].astype(F32)
        edges_1[side] = group[:, 15 * side, :].astype(BF16)
    for copy in last_rims[2:]:
        copy.start()
    last_rows((6, 7, 8, 14))
    for copy in last_rims:
        copy.wait()
    close_rims(padded_1, rims_1)
    last_rows((0, 15), closing=True)
    sixteen = iota((16, 1), 0)

    def patch(row, _):
        left = saved[0, row] + jnp.where(sixteen == 0, ends[0, pl.ds(row, 1), :], 0.0)
        right = saved[1, row] + jnp.where(sixteen == 15, ends[1, pl.ds(row, 1), :], 0.0)

        @on_air
        def _():
            out_ref[row, 0:16, :] = left.astype(BF16)
            out_ref[row, COLS - 16 : COLS, :] = right.astype(BF16)

        @on_sea
        def _():
            out_ref[row, 0:16, :] = (left * mask[row, 0:16, :].astype(F32)).astype(BF16)
            out_ref[row, COLS - 16 : COLS, :] = (right * mask[row, COLS - 16 : COLS, :].astype(F32)).astype(BF16)

        return 0

    lax.fori_loop(0, ROWS, patch, 0)


def body(
    state,
    intersection_lists,
    intersection_matrices,
    water_indicator,
    atmosphere_kernels,
    ocean_kernels,
    flux_projection,
    coupling_matrix,
):
    dma = pltpu.SemaphoreType.DMA
    vmem = pl.BlockSpec(memory_space=pltpu.VMEM)
    hbm = pl.BlockSpec(memory_space=pl.ANY)
    tables = pltpu.VMEM((8, SLOT_TOTAL), jnp.int32)
    scalars = pltpu.SMEM((8, SLOT_TOTAL), jnp.int32)
    slots = [pltpu.VMEM((SLOT_TOTAL, *piece), BF16) for piece in PIECES]
    dense = [pltpu.VMEM((32, *piece), BF16) for piece in PIECES]
    result = pl.pallas_call(
        step_kernel,
        out_shape=pltpu.VMEM((ROWS, COLS, WIDE), BF16),
        in_specs=[vmem, hbm, hbm, vmem, hbm, hbm, hbm, hbm],
        out_specs=vmem,
        scratch_shapes=slots
        + slots
        + dense
        + dense
        + [
            pltpu.VMEM((ROWS, COLS, WIDE), BF16),
            pltpu.VMEM((ENTRIES, BLOCK, BLOCK), BF16),
            pltpu.VMEM((WIDE, HALF), BF16),
            pltpu.VMEM((HALF, WIDE), BF16),
            pltpu.VMEM((3, 3, WIDE, WIDE), BF16),
            pltpu.VMEM((3, 3, HALF, HALF), BF16),
            pltpu.VMEM((32, BLOCK, HALF), BF16),
            pltpu.VMEM((ROWS, COLS, WIDE), BF16),
            pltpu.VMEM((SLOT_TOTAL, 32, HALF), F32),
            pltpu.VMEM((ROWS, COLS, WIDE), F32),
            pltpu.VMEM((ROWS + 2, COLS, WIDE), BF16),
            pltpu.VMEM((ROWS + 2, COLS, WIDE), BF16),
            pltpu.VMEM((2, 16, WIDE), BF16),
            pltpu.VMEM((2, 16, WIDE), BF16),
            pltpu.VMEM((2, 3, 16, WIDE), BF16),
            pltpu.VMEM((2, 3, 16, WIDE), BF16),
            pltpu.VMEM((2, 24, WIDE), F32),
            pltpu.VMEM((2, 16, WIDE), F32),
            pltpu.VMEM((2, ROWS, 16, WIDE), F32),
            pltpu.VMEM((1, SLOT_TOTAL), jnp.int32),
            pltpu.VMEM((TILES, 1, SLOT_TOTAL), jnp.int32),
            tables,
            scalars,
            tables,
            scalars,
            dma((6,)),
            dma((3,)),
            dma((N,)),
            dma((N,)),
            dma((N,)),
            dma((2,)),
            dma((N, 2)),
            dma((N, 2)),
            dma((2, 8)),
            dma((2, 8)),
        ],
        compiler_params=pltpu.CompilerParams(
            collective_id=0, has_side_effects=True, vmem_limit_bytes=58 << 20
        ),
    )(
        intersection_lists.reshape(3, 1, ENTRIES),
        state[0],
        intersection_matrices.reshape(ENTRIES, BLOCK, BLOCK),
        water_indicator,
        atmosphere_kernels,
        ocean_kernels,
        flux_projection,
        coupling_matrix,
    )
    return result[None]


def solution(mesh):
    placed = (
        P("grp", "lat", "lon", None),
        P("grp", "lat", "lon", None, None),
        P("grp", "lat", "lon", None, None, None),
        P("lat", "lon"),
        P(),
        P(),
        P(),
        P(),
    )
    return jax.shard_map(
        body, mesh=mesh, in_specs=placed, out_specs=P("grp", "lat", "lon", None), check_vma=False
    )
```

```python
import jax
import jax.numpy as jnp
from jax import lax
from jax.experimental import pallas as pl
from jax.experimental.pallas import tpu as pltpu
from jax.sharding import PartitionSpec as P

ROWS = 16
COLS = 128
WIDE = 512
HALF = 256
BLOCK = 128
ENTRIES = 64
TILES = 64
SLOT_TOTAL = 2 * TILES
CHUNKS = tuple((row, 1, 0, 256) for row in range(7)) + ((7, 1, 0, 128), (7, 1, 128, 128))
PIECES = tuple((16 * chunk[1], chunk[3]) for chunk in CHUNKS)
N = len(CHUNKS)
MESH = pl.DeviceIdType.MESH
F32 = jnp.float32
BF16 = jnp.bfloat16


def dot(a, b):
    return jnp.dot(a, b, preferred_element_type=F32)


def iota(shape, dim):
    return lax.broadcasted_iota(jnp.int32, shape, dim)


def ones_where(condition):
    return condition.astype(F32).astype(BF16)


def silu(value):
    return value / (1.0 + jnp.exp(-value))


def activated(value):
    return silu(value.astype(F32)).astype(BF16)


def place_entries(lists, labels, places):
    down, across = iota((ENTRIES, ENTRIES), 0), iota((ENTRIES, ENTRIES), 1)

    def column(row):
        return jnp.sum(jnp.where(down == across, row, 0), axis=1, keepdims=True)

    owner_row = lists[0]
    owner, source, target = column(owner_row), column(lists[1]), column(lists[2])
    rank = jnp.sum(((owner_row == owner) & (across < down)).astype(jnp.int32), axis=1, keepdims=True)
    slot = 2 * jnp.bitwise_xor(owner, 8) + rank
    hit = slot == iota((ENTRIES, SLOT_TOTAL), 1)
    entry = jnp.sum(jnp.where(hit, iota((ENTRIES, SLOT_TOTAL), 0), 0), axis=0, keepdims=True)
    taken = jnp.sum(jnp.where(hit, source, 0), axis=0, keepdims=True)
    labels[...] = jnp.sum(jnp.where(hit, target + 1, 0), axis=0, keepdims=True) - 1
    places[...] = jnp.concatenate([entry, taken] * 4, axis=0)


def sort_slots(labels_ref, me, orders):
    labels = labels_ref[...].reshape(TILES, SLOT_TOTAL)
    lane = iota((TILES, SLOT_TOTAL), 1)
    first = jnp.sum(jnp.where(lane == 2 * me, labels, 0), axis=1, keepdims=True)
    second = jnp.sum(jnp.where(lane == 2 * me + 1, labels, 0), axis=1, keepdims=True)
    column = jnp.concatenate([first, second], axis=0)
    down, across = iota((SLOT_TOTAL, SLOT_TOTAL), 0), iota((SLOT_TOTAL, SLOT_TOTAL), 1)
    keys = jnp.broadcast_to(column, (SLOT_TOTAL, SLOT_TOTAL))
    row = jnp.sum(jnp.where(down == across, keys, 0), axis=0, keepdims=True)
    other = jnp.broadcast_to(row, (SLOT_TOTAL, SLOT_TOTAL))
    ahead = (other < keys) | ((other == keys) & (across < down))
    rank = jnp.sum(ahead.astype(jnp.int32), axis=1, keepdims=True)
    hit = rank == across
    slot = 2 * (down % TILES) + down // TILES
    order = jnp.sum(jnp.where(hit, slot, 0), axis=0, keepdims=True)
    sorted_keys = jnp.sum(jnp.where(hit, keys, 0), axis=0, keepdims=True)
    previous = jnp.sum(jnp.where(rank + 1 == across, keys, 0), axis=0, keepdims=True)
    opens = ((sorted_keys != previous) | (iota((1, SLOT_TOTAL), 1) == 0)).astype(jnp.int32)
    count = jnp.sum((keys == across).astype(jnp.int32), axis=0, keepdims=True)
    last = jnp.sum((keys <= across).astype(jnp.int32), axis=0, keepdims=True) - 1
    last = jnp.maximum(last, 0)
    orders[...] = jnp.concatenate([order, opens, last, count] * 2, axis=0)


def air_blocks(state, projection, blocks):
    for row in range(ROWS):
        flux = dot(state[row], projection[...]).astype(BF16)
        band, sub = row // 8, row % 8
        blocks[8 * band : 8 * band + 8, 16 * sub : 16 * sub + 16, :] = flux.reshape(8, 16, HALF)


def sea_blocks(state, water, mask, halves, blocks):
    cell, pair = iota((COLS, 2 * COLS), 1), iota((COLS, 2 * COLS), 0)
    ones = jnp.ones((2 * COLS, HALF), F32).astype(BF16)
    for row in range(ROWS):
        band, sub = row // 8, row % 8
        for side in range(2):
            wet = jnp.where(cell == 2 * pair + side, water[row : row + 1, :], 0).astype(F32).astype(BF16)
            wet = dot(wet, ones)
            lanes = slice(side * HALF, (side + 1) * HALF)
            mask[row, :, lanes] = wet.astype(BF16)
            surface = (state[row, :, lanes].astype(F32) * wet).reshape(16, 8, HALF)
            start = 64 * side + 8 * sub
            for b in range(16):
                halves[4 * (16 * band + b) + start // 32, start % 32 : start % 32 + 8, :] = surface[b]
    cell, place = iota((BLOCK, BLOCK), 0), iota((BLOCK, BLOCK), 1)
    order = ones_where((cell % 2) * 64 + (cell // 16) * 8 + (cell % 16) // 2 == place)

    def one(b, _):
        blocks[b] = dot(order, halves[pl.ds(4 * b, 4)].reshape(BLOCK, HALF).astype(BF16)).astype(BF16)
        return 0

    lax.fori_loop(0, 32, one, 0, unroll=4)


def moved_east(value):
    return jnp.where(iota((COLS, 1), 0) == 0, 0.0, pltpu.roll(value, 1, 0))


def moved_west(value):
    return jnp.where(iota((COLS, 1), 0) == COLS - 1, 0.0, pltpu.roll(value, COLS - 1, 0))


def total(terms):
    result = terms[0]
    for term in terms[1:]:
        result = result + term
    return result


def row_parts(value):
    return [value[i * COLS : (i + 1) * COLS] for i in range(value.shape[0] // COLS)]


def mix_air(windows, kernel, sides=None):
    left = right = windows
    if sides is not None:
        left, right = ([jnp.concatenate(pair, axis=0) for pair in zip(windows, side)] for side in sides)
    west = total([dot(left[r], kernel[r, 0]) for r in range(3)])
    here = total([dot(windows[r], kernel[r, 1]) for r in range(3)])
    east = total([dot(right[r], kernel[r, 2]) for r in range(3)])
    rows = [a + moved_east(b) + moved_west(c) for a, b, c in zip(*map(row_parts, (here, west, east)))]
    if sides is None:
        return rows
    size = here.shape[0]
    return rows, (west[size:], east[size:])


def mix_sea(windows, kernel, sides=None):
    even = [window[:, :HALF] for window in windows]
    odd = [window[:, HALF:] for window in windows]
    left, right = odd, even
    if sides is not None:
        left = [jnp.concatenate([a, b[:, HALF:]], axis=0) for a, b in zip(odd, sides[0])]
        right = [jnp.concatenate([a, b[:, :HALF]], axis=0) for a, b in zip(even, sides[1])]
    low = total([dot(even[r], kernel[r, 1]) + dot(odd[r], kernel[r, 2]) for r in range(3)])
    high = total([dot(even[r], kernel[r, 0]) + dot(odd[r], kernel[r, 1]) for r in range(3)])
    west = total([dot(left[r], kernel[r, 0]) for r in range(3)])
    east = total([dot(right[r], kernel[r, 2]) for r in range(3)])
    rows = [
        jnp.concatenate([a + moved_east(c), b + moved_west(d)], axis=1)
        for a, b, c, d in zip(*map(row_parts, (low, high, west, east)))
    ]
    if sides is None:
        return rows
    size = low.shape[0]
    nothing = jnp.zeros((ROWS, HALF), F32)
    ends = jnp.concatenate([west[size:], nothing], axis=1), jnp.concatenate([nothing, east[size:]], axis=1)
    return rows, ends


def step_kernel(
    lists, state_in, factors_in, water, air_in, sea_in, projection_in, coupling_in, out_ref, *scratch
):
    send, scratch = scratch[:N], scratch[N:]
    recv, scratch = scratch[:N], scratch[N:]
    leaving, scratch = scratch[:N], scratch[N:]
    arriving, scratch = scratch[:N], scratch[N:]
    (state, factors, projection, coupling, air, sea, blocks, mask, sums, acc) = scratch[:10]
    (padded_0, padded_1, edges_0, edges_1, rims_0, rims_1, sides, ends, saved) = scratch[10:19]
    (labels, marks, places, place_table, orders, order_table) = scratch[19:25]
    (fetch, local_sem, own, sent, landed, mark_sem, over_sent, over_landed, rim_sent, rim_landed) = scratch[25:]

    grp, lat, lon = lax.axis_index("grp"), lax.axis_index("lat"), lax.axis_index("lon")
    me = lat * 16 + lon
    high, x, core = lon // 8, (lon // 2) % 4, lon % 2
    facing = (1 - grp, lat, (lon + 8) % 16)
    west, east = (lon + 15) % 16, (lon + 1) % 16
    north, south = (lat + 3) % 4, (lat + 1) % 4

    def target(k):
        z = (lat + k) % 4
        y = (high + k // 16 + k // 2) % 2
        c = (core + k // 32 + k) % 2
        return z, y * 8 + ((x + k // 4 + k) % 4) * 2 + c

    get_state = pltpu.make_async_copy(state_in, state, fetch.at[0])
    get_factors = pltpu.make_async_copy(factors_in, factors, fetch.at[1])
    get_projection = pltpu.make_async_copy(projection_in, projection, fetch.at[2])
    get_coupling = pltpu.make_async_copy(coupling_in, coupling, fetch.at[3])
    get_air = [pltpu.make_async_copy(air_in.at[layer], air, fetch.at[4 + layer]) for layer in range(2)]
    get_sea = [pltpu.make_async_copy(sea_in.at[layer], sea, fetch.at[4 + layer]) for layer in range(2)]
    get_state.start()
    get_projection.start()
    get_factors.start()
    get_coupling.start()

    def on_air(body):
        pl.when(grp == 0)(body)

    def on_sea(body):
        pl.when(grp == 1)(body)

    on_air(get_air[0].start)
    on_sea(get_sea[0].start)

    barrier = pltpu.get_barrier_semaphore()

    def greet(k, _):
        z, j = target(k)
        pl.semaphore_signal(barrier, inc=1, device_id=(grp, z, j), device_id_type=MESH)
        return 0

    lax.fori_loop(1, TILES, greet, 0)
    pl.semaphore_signal(barrier, inc=1, device_id=facing, device_id_type=MESH)

    place_entries(lists, labels, places)
    tell = pltpu.make_async_copy(places, place_table, local_sem.at[0])
    tell.start()

    def rim_copies(layer, padded, edges, rims):
        pushes = [(padded.at[1], padded.at[17], north, lon), (padded.at[16], padded.at[0], south, lon)]
        for side, j in ((0, west), (1, east)):
            for z, place in ((north, 2), (lat, 1), (south, 0)):
                pushes.append((edges.at[side], rims.at[1 - side, place], z, j))
        return [
            pltpu.make_async_remote_copy(
                source,
                goal,
                rim_sent.at[layer, index],
                rim_landed.at[layer, index],
                device_id=(grp, z, j),
                device_id_type=MESH,
            )
            for index, (source, goal, z, j) in enumerate(pushes)
        ]

    get_state.wait()

    @on_air
    def _():
        get_projection.wait()
        air_blocks(state, projection, blocks)

    @on_sea
    def _():
        get_projection.wait()
        sea_blocks(state, water, mask, sums, blocks)

    get_factors.wait()
    tell.wait()

    def payload(slot, start, length):
        factor = factors[place_table[0, slot], start : start + length, :]
        return dot(factor, blocks[place_table[1, slot]]).astype(BF16)

    def own_copy(chunk):
        mine = pl.ds(2 * me, 2)
        return pltpu.make_async_copy(send[chunk].at[mine], recv[chunk].at[mine], own.at[chunk])

    def start_send(chunk, k):
        z, j = target(k)
        pltpu.make_async_remote_copy(
            send[chunk].at[pl.ds(2 * (z * 16 + j), 2)],
            recv[chunk].at[pl.ds(2 * me, 2)],
            sent.at[chunk],
            landed.at[chunk],
            device_id=(grp, z, j),
            device_id_type=MESH,
        ).start()

    def send_payloads(chunk):
        def one(k, _):
            start_send(chunk, k)
            return 0

        lax.fori_loop(1, TILES, one, 0)
        own_copy(chunk).start()

    def first_payloads(k):
        z, j = target(k)
        for i in range(2):
            slot = 2 * (z * 16 + j) + i
            send[0][slot] = payload(slot, 0, PIECES[0][0])

    def first_step(k, _):
        first_payloads(k)
        start_send(0, k - 1)
        return 0

    padded_0[1] = activated(state[0])
    padded_0[16] = activated(state[ROWS - 1])
    for side, first in ((0, 0), (1, COLS - 16)):
        group = silu(state[:, first : first + 16, :].astype(F32))
        edges_0[side] = group[:, 15 * side, :].astype(BF16)
    first_rims = rim_copies(0, padded_0, edges_0, rims_0)

    pl.semaphore_wait(barrier, TILES)
    def send_label(k, _):
        z, j = target(k)
        pltpu.make_async_remote_copy(
            labels, marks.at[me], mark_sem.at[0], mark_sem.at[1], device_id=(grp, z, j), device_id_type=MESH
        ).start()
        return 0

    lax.fori_loop(1, TILES, send_label, 0)
    own_label = pltpu.make_async_copy(labels, marks.at[me], local_sem.at[1])
    own_label.start()

    for copy in first_rims:
        copy.start()

    first_payloads(0)
    first_payloads(1)
    lax.fori_loop(2, TILES, first_step, 0, unroll=2)
    start_send(0, TILES - 1)
    own_copy(0).start()

    later = 16 * CHUNKS[1][0]

    def later_payloads(slot, _):
        value = payload(slot, later, BLOCK - later)
        for chunk in range(1, N):
            first, count, lane, lanes = CHUNKS[chunk]
            start = 16 * first - later
            send[chunk][slot] = value[start : start + 16 * count, lane : lane + lanes]
        return 0

    lax.fori_loop(0, SLOT_TOTAL, later_payloads, 0, unroll=8)
    for chunk in range(1, 2):
        send_payloads(chunk)

    def activate(row, _):
        padded_0[row + 1] = activated(state[row])
        return 0

    lax.fori_loop(1, ROWS - 1, activate, 0, unroll=2)
    for copy in first_rims:
        copy.wait()

    def close_rims(padded, rims):
        @pl.when(lat == 0)
        def _():
            padded[0] = jnp.zeros((COLS, WIDE), BF16)

        @pl.when(lat == 3)
        def _():
            padded[17] = jnp.zeros((COLS, WIDE), BF16)

        for side in range(2):
            sides[side, 0:1, :] = rims[side, 0].astype(F32)[15:16] * jnp.where(lat == 0, 0.0, 1.0)
            sides[side, 1:17, :] = rims[side, 1].astype(F32)
            sides[side, 17:18, :] = rims[side, 2].astype(F32)[0:1] * jnp.where(lat == 3, 0.0, 1.0)

    def end_columns():
        @on_air
        def _():
            for side, tap in ((0, 0), (1, 2)):
                ends[side] = total([dot(sides[side, r : r + 16, :].astype(BF16), air[r, tap]) for r in range(3)])

        @on_sea
        def _():
            nothing = jnp.zeros((ROWS, HALF), F32)
            first = total([dot(sides[0, r : r + 16, HALF:].astype(BF16), sea[r, 0]) for r in range(3)])
            final = total([dot(sides[1, r : r + 16, :HALF].astype(BF16), sea[r, 2]) for r in range(3)])
            ends[0] = jnp.concatenate([first, nothing], axis=1)
            ends[1] = jnp.concatenate([nothing, final], axis=1)

    def mixed_rows(mix, kernel):
        def some_rows(step, _):
            windows = [padded_0[pl.ds(4 * step + r, 4)].reshape(4 * COLS, WIDE) for r in range(3)]
            for i, value in enumerate(mix(windows, kernel)):
                acc[4 * step + i] = value + state[4 * step + i].astype(F32)
            return 0

        lax.fori_loop(0, 4, some_rows, 0)

    close_rims(padded_0, rims_0)

    @on_air
    def _():
        get_air[0].wait()
        mixed_rows(mix_air, air)

    @on_sea
    def _():
        get_sea[0].wait()
        mixed_rows(mix_sea, sea)

    end_columns()
    eight = iota((8, 1), 0)

    def add_ends(row, _):
        acc[row, 0:8, :] += jnp.where(eight == 0, ends[0, pl.ds(row, 1), :], 0.0)
        acc[row, COLS - 8 : COLS, :] += jnp.where(eight == 7, ends[1, pl.ds(row, 1), :], 0.0)
        return 0

    lax.fori_loop(0, ROWS, add_ends, 0)
    on_air(get_air[1].start)
    on_sea(get_sea[1].start)
    get_coupling.wait()

    own_label.wait()
    others = pltpu.make_async_remote_copy(
        marks.at[pl.ds(0, TILES - 1)],
        marks.at[pl.ds(0, TILES - 1)],
        mark_sem.at[0],
        mark_sem.at[1],
        device_id=facing,
        device_id_type=MESH,
    )
    others.wait_recv()
    others.wait_send()
    sort_slots(marks, me, orders)
    tell_order = pltpu.make_async_copy(orders, order_table, local_sem.at[2])
    tell_order.start()
    tell_order.wait()

    def crossing(chunk, part):
        half = pl.ds(16 * part, 16)
        return pltpu.make_async_remote_copy(
            leaving[chunk].at[half],
            arriving[chunk].at[half],
            over_sent.at[chunk, part],
            over_landed.at[chunk, part],
            device_id=facing,
            device_id_type=MESH,
        )

    next_sends = [(c + 2,) if c + 2 < N else () for c in range(N)]

    def sum_and_cross(chunk):
        piece, lanes = PIECES[chunk]
        own_copy(chunk).wait()
        rest = pl.ds(0, SLOT_TOTAL - 2)
        everyone = pltpu.make_async_remote_copy(
            send[chunk].at[rest],
            recv[chunk].at[rest],
            sent.at[chunk],
            landed.at[chunk],
            device_id=facing,
            device_id_type=MESH,
        )
        everyone.wait_recv()
        everyone.wait_send()
        for following in next_sends[chunk]:
            send_payloads(following)

        def accumulate(p, running):
            value = recv[chunk][order_table[0, p]].astype(F32)
            running = jnp.where(order_table[1, p] == 1, 0.0, running) + value
            sums[p, 0:piece, 0:lanes] = running
            return running

        lax.fori_loop(0, SLOT_TOTAL, accumulate, jnp.zeros((piece, lanes), F32), unroll=8)

        def settle(b, _):
            value = jnp.where(order_table[3, b] > 0, sums[order_table[2, b], 0:piece, 0:lanes], 0.0)
            leaving[chunk][b] = value.astype(BF16)
            return 0

        lax.fori_loop(0, 32, settle, 0, unroll=4)
        crossing(chunk, 0).start()
        on_air(crossing(chunk, 1).start)

    def finish_rows(*chunks):
        for chunk in chunks:
            crossing(chunk, 0).wait()
            on_air(crossing(chunk, 1).wait_send)
            on_sea(crossing(chunk, 1).wait_recv)
        first, count = CHUNKS[chunks[0]][:2]
        wanted = [(band, i, 8 * band + first + i) for band in (1, 0) for i in range(count)]

        def given(band, i, blocks_across):
            here = slice(blocks_across * band, blocks_across * (band + 1))
            parts = [arriving[chunk][here, 16 * i : 16 * i + 16, :] for chunk in chunks]
            parts = [part.reshape(16 * blocks_across, part.shape[2]) for part in parts]
            return parts[0] if len(parts) == 1 else jnp.concatenate(parts, axis=1)

        @on_air
        def _():
            for band, i, row in wanted:
                value = (acc[row] + dot(given(band, i, 8), coupling[...])).astype(BF16)
                state[row] = value
                padded_1[row + 1] = activated(value)

        @on_sea
        def _():
            cell, pair = iota((COLS, 2 * COLS), 1), iota((COLS, 2 * COLS), 0)
            for band, i, row in wanted:
                force = given(band, i, 16)
                parts = [dot(ones_where(cell == 2 * pair + side), force) for side in range(2)]
                value = (acc[row] + jnp.concatenate(parts, axis=1)) * mask[row].astype(F32)
                value = value.astype(BF16)
                state[row] = value
                padded_1[row + 1] = activated(value)

    def last_rows(rows, closing=False):
        def windows():
            return [jnp.concatenate([padded_1[row + r] for row in rows], axis=0) for r in range(3)]

        def mixed(mix, kernel):
            if not closing:
                return mix(windows(), kernel)
            rims = [[sides[side, r : r + 16, :].astype(BF16) for r in range(3)] for side in range(2)]
            values, (first, final) = mix(windows(), kernel, rims)
            ends[0] = first
            ends[1] = final
            return values

        def put(row, value, wet):
            value = value + state[row].astype(F32)
            saved[0, row] = value[0:16]
            saved[1, row] = value[COLS - 16 : COLS]
            out_ref[row] = (value if wet is None else value * wet).astype(BF16)

        @on_air
        def _():
            for row, value in zip(rows, mixed(mix_air, air)):
                put(row, value, None)

        @on_sea
        def _():
            for row, value in zip(rows, mixed(mix_sea, sea)):
                put(row, value, mask[row].astype(F32))

    last_rims = rim_copies(1, padded_1, edges_1, rims_1)
    sum_and_cross(0)
    sum_and_cross(1)
    finish_rows(0)
    last_rims[0].start()
    for chunk in range(2, 6):
        sum_and_cross(chunk)
        finish_rows(chunk - 1)
    on_air(get_air[1].wait)
    on_sea(get_sea[1].wait)
    sum_and_cross(6)
    finish_rows(5)
    last_rows((1, 2, 3, 4))
    sum_and_cross(7)
    last_rows((9, 10, 11, 12))
    sum_and_cross(8)
    finish_rows(6)
    last_rows((5, 13))
    finish_rows(7, 8)
    last_rims[1].start()
    for side, first in ((0, 0), (1, COLS - 16)):
        group = padded_1[1:17, first : first + 16, :].astype(F32)
        edges_1[side] = group[:, 15 * side, :].astype(BF16)
    for copy in last_rims[2:]:
        copy.start()
    last_rows((6, 7, 8, 14))
    for copy in last_rims:
        copy.wait()
    close_rims(padded_1, rims_1)
    last_rows((0, 15), closing=True)
    sixteen = iota((16, 1), 0)

    def patch(row, _):
        left = saved[0, row] + jnp.where(sixteen == 0, ends[0, pl.ds(row, 1), :], 0.0)
        right = saved[1, row] + jnp.where(sixteen == 15, ends[1, pl.ds(row, 1), :], 0.0)

        @on_air
        def _():
            out_ref[row, 0:16, :] = left.astype(BF16)
            out_ref[row, COLS - 16 : COLS, :] = right.astype(BF16)

        @on_sea
        def _():
            out_ref[row, 0:16, :] = (left * mask[row, 0:16, :].astype(F32)).astype(BF16)
            out_ref[row, COLS - 16 : COLS, :] = (right * mask[row, COLS - 16 : COLS, :].astype(F32)).astype(BF16)

        return 0

    lax.fori_loop(0, ROWS, patch, 0)


def body(
    state,
    intersection_lists,
    intersection_matrices,
    water_indicator,
    atmosphere_kernels,
    ocean_kernels,
    flux_projection,
    coupling_matrix,
):
    dma = pltpu.SemaphoreType.DMA
    vmem = pl.BlockSpec(memory_space=pltpu.VMEM)
    hbm = pl.BlockSpec(memory_space=pl.ANY)
    tables = pltpu.VMEM((8, SLOT_TOTAL), jnp.int32)
    scalars = pltpu.SMEM((8, SLOT_TOTAL), jnp.int32)
    slots = [pltpu.VMEM((SLOT_TOTAL, *piece), BF16) for piece in PIECES]
    dense = [pltpu.VMEM((32, *piece), BF16) for piece in PIECES]
    result = pl.pallas_call(
        step_kernel,
        out_shape=pltpu.VMEM((ROWS, COLS, WIDE), BF16),
        in_specs=[vmem, hbm, hbm, vmem, hbm, hbm, hbm, hbm],
        out_specs=vmem,
        scratch_shapes=slots
        + slots
        + dense
        + dense
        + [
            pltpu.VMEM((ROWS, COLS, WIDE), BF16),
            pltpu.VMEM((ENTRIES, BLOCK, BLOCK), BF16),
            pltpu.VMEM((WIDE, HALF), BF16),
            pltpu.VMEM((HALF, WIDE), BF16),
            pltpu.VMEM((3, 3, WIDE, WIDE), BF16),
            pltpu.VMEM((3, 3, HALF, HALF), BF16),
            pltpu.VMEM((32, BLOCK, HALF), BF16),
            pltpu.VMEM((ROWS, COLS, WIDE), BF16),
            pltpu.VMEM((SLOT_TOTAL, 32, HALF), F32),
            pltpu.VMEM((ROWS, COLS, WIDE), F32),
            pltpu.VMEM((ROWS + 2, COLS, WIDE), BF16),
            pltpu.VMEM((ROWS + 2, COLS, WIDE), BF16),
            pltpu.VMEM((2, 16, WIDE), BF16),
            pltpu.VMEM((2, 16, WIDE), BF16),
            pltpu.VMEM((2, 3, 16, WIDE), BF16),
            pltpu.VMEM((2, 3, 16, WIDE), BF16),
            pltpu.VMEM((2, 24, WIDE), F32),
            pltpu.VMEM((2, 16, WIDE), F32),
            pltpu.VMEM((2, ROWS, 16, WIDE), F32),
            pltpu.VMEM((1, SLOT_TOTAL), jnp.int32),
            pltpu.VMEM((TILES, 1, SLOT_TOTAL), jnp.int32),
            tables,
            scalars,
            tables,
            scalars,
            dma((6,)),
            dma((3,)),
            dma((N,)),
            dma((N,)),
            dma((N,)),
            dma((2,)),
            dma((N, 2)),
            dma((N, 2)),
            dma((2, 8)),
            dma((2, 8)),
        ],
        compiler_params=pltpu.CompilerParams(
            collective_id=0, has_side_effects=True, vmem_limit_bytes=58 << 20
        ),
    )(
        intersection_lists.reshape(3, 1, ENTRIES),
        state[0],
        intersection_matrices.reshape(ENTRIES, BLOCK, BLOCK),
        water_indicator,
        atmosphere_kernels,
        ocean_kernels,
        flux_projection,
        coupling_matrix,
    )
    return result[None]


def solution(mesh):
    placed = (
        P("grp", "lat", "lon", None),
        P("grp", "lat", "lon", None, None),
        P("grp", "lat", "lon", None, None, None),
        P("lat", "lon"),
        P(),
        P(),
        P(),
        P(),
    )
    return jax.shard_map(
        body, mesh=mesh, in_specs=placed, out_specs=P("grp", "lat", "lon", None), check_vma=False
    )
```

```python
import jax
import jax.numpy as jnp
from jax import lax
from jax.experimental import pallas as pl
from jax.experimental.pallas import tpu as pltpu
from jax.sharding import PartitionSpec as P

ROWS = 16
COLS = 128
WIDE = 512
HALF = 256
BLOCK = 128
ENTRIES = 64
TILES = 64
SLOT_TOTAL = 2 * TILES
CHUNKS = tuple((row, 1, 0, 256) for row in (0, 1, 7, 6, 2, 5, 3)) + ((4, 1, 0, 128), (4, 1, 128, 128))
PIECES = tuple((16 * chunk[1], chunk[3]) for chunk in CHUNKS)
N = len(CHUNKS)
MESH = pl.DeviceIdType.MESH
F32 = jnp.float32
BF16 = jnp.bfloat16


def dot(a, b):
    return jnp.dot(a, b, preferred_element_type=F32)


def iota(shape, dim):
    return lax.broadcasted_iota(jnp.int32, shape, dim)


def ones_where(condition):
    return condition.astype(F32).astype(BF16)


def silu(value):
    return value / (1.0 + jnp.exp(-value))


def activated(value):
    return silu(value.astype(F32)).astype(BF16)


def place_entries(lists, labels, places):
    down, across = iota((ENTRIES, ENTRIES), 0), iota((ENTRIES, ENTRIES), 1)

    def column(row):
        return jnp.sum(jnp.where(down == across, row, 0), axis=1, keepdims=True)

    owner_row = lists[0]
    owner, source, target = column(owner_row), column(lists[1]), column(lists[2])
    rank = jnp.sum(((owner_row == owner) & (across < down)).astype(jnp.int32), axis=1, keepdims=True)
    slot = 2 * jnp.bitwise_xor(owner, 8) + rank
    hit = slot == iota((ENTRIES, SLOT_TOTAL), 1)
    entry = jnp.sum(jnp.where(hit, iota((ENTRIES, SLOT_TOTAL), 0), 0), axis=0, keepdims=True)
    taken = jnp.sum(jnp.where(hit, source, 0), axis=0, keepdims=True)
    labels[...] = jnp.sum(jnp.where(hit, target + 1, 0), axis=0, keepdims=True) - 1
    places[...] = jnp.concatenate([entry, taken] * 4, axis=0)


def sort_slots(labels_ref, me, orders):
    labels = labels_ref[...].reshape(TILES, SLOT_TOTAL)
    lane = iota((TILES, SLOT_TOTAL), 1)
    first = jnp.sum(jnp.where(lane == 2 * me, labels, 0), axis=1, keepdims=True)
    second = jnp.sum(jnp.where(lane == 2 * me + 1, labels, 0), axis=1, keepdims=True)
    column = jnp.concatenate([first, second], axis=0)
    down, across = iota((SLOT_TOTAL, SLOT_TOTAL), 0), iota((SLOT_TOTAL, SLOT_TOTAL), 1)
    keys = jnp.broadcast_to(column, (SLOT_TOTAL, SLOT_TOTAL))
    row = jnp.sum(jnp.where(down == across, keys, 0), axis=0, keepdims=True)
    other = jnp.broadcast_to(row, (SLOT_TOTAL, SLOT_TOTAL))
    ahead = (other < keys) | ((other == keys) & (across < down))
    rank = jnp.sum(ahead.astype(jnp.int32), axis=1, keepdims=True)
    hit = rank == across
    slot = 2 * (down % TILES) + down // TILES
    order = jnp.sum(jnp.where(hit, slot, 0), axis=0, keepdims=True)
    sorted_keys = jnp.sum(jnp.where(hit, keys, 0), axis=0, keepdims=True)
    previous = jnp.sum(jnp.where(rank + 1 == across, keys, 0), axis=0, keepdims=True)
    opens = ((sorted_keys != previous) | (iota((1, SLOT_TOTAL), 1) == 0)).astype(jnp.int32)
    count = jnp.sum((keys == across).astype(jnp.int32), axis=0, keepdims=True)
    last = jnp.sum((keys <= across).astype(jnp.int32), axis=0, keepdims=True) - 1
    last = jnp.maximum(last, 0)
    orders[...] = jnp.concatenate([order, opens, last, count] * 2, axis=0)


def air_blocks(state, projection, blocks):
    for row in range(ROWS):
        flux = dot(state[row], projection[...]).astype(BF16)
        band, sub = row // 8, row % 8
        blocks[8 * band : 8 * band + 8, 16 * sub : 16 * sub + 16, :] = flux.reshape(8, 16, HALF)


def sea_blocks(state, water, mask, halves, blocks):
    cell, pair = iota((COLS, 2 * COLS), 1), iota((COLS, 2 * COLS), 0)
    ones = jnp.ones((2 * COLS, HALF), F32).astype(BF16)
    for row in range(ROWS):
        band, sub = row // 8, row % 8
        for side in range(2):
            wet = jnp.where(cell == 2 * pair + side, water[row : row + 1, :], 0).astype(F32).astype(BF16)
            wet = dot(wet, ones)
            lanes = slice(side * HALF, (side + 1) * HALF)
            mask[row, :, lanes] = wet.astype(BF16)
            surface = (state[row, :, lanes].astype(F32) * wet).reshape(16, 8, HALF)
            start = 64 * side + 8 * sub
            for b in range(16):
                halves[4 * (16 * band + b) + start // 32, start % 32 : start % 32 + 8, :] = surface[b]
    cell, place = iota((BLOCK, BLOCK), 0), iota((BLOCK, BLOCK), 1)
    order = ones_where((cell % 2) * 64 + (cell // 16) * 8 + (cell % 16) // 2 == place)

    def one(b, _):
        blocks[b] = dot(order, halves[pl.ds(4 * b, 4)].reshape(BLOCK, HALF).astype(BF16)).astype(BF16)
        return 0

    lax.fori_loop(0, 32, one, 0, unroll=4)


def moved_east(value):
    return jnp.where(iota((COLS, 1), 0) == 0, 0.0, pltpu.roll(value, 1, 0))


def moved_west(value):
    return jnp.where(iota((COLS, 1), 0) == COLS - 1, 0.0, pltpu.roll(value, COLS - 1, 0))


def total(terms):
    result = terms[0]
    for term in terms[1:]:
        result = result + term
    return result


def row_parts(value):
    return [value[i * COLS : (i + 1) * COLS] for i in range(value.shape[0] // COLS)]


def mix_air(taps, kernel, sides=None):
    left = right = taps
    if sides is not None:
        left, right = (
            [(r, jnp.concatenate([window, extra], axis=0)) for (r, window), extra in zip(taps, side)]
            for side in sides
        )
    west = total([dot(window, kernel[r, 0]) for r, window in left])
    here = total([dot(window, kernel[r, 1]) for r, window in taps])
    east = total([dot(window, kernel[r, 2]) for r, window in right])
    rows = [a + moved_east(b) + moved_west(c) for a, b, c in zip(*map(row_parts, (here, west, east)))]
    if sides is None:
        return rows
    size = here.shape[0]
    return rows, (west[size:], east[size:])


def mix_sea(taps, kernel, sides=None):
    even = [(r, window[:, :HALF]) for r, window in taps]
    odd = [(r, window[:, HALF:]) for r, window in taps]
    left, right = odd, even
    if sides is not None:
        left = [(r, jnp.concatenate([a, b[:, HALF:]], axis=0)) for (r, a), b in zip(odd, sides[0])]
        right = [(r, jnp.concatenate([a, b[:, :HALF]], axis=0)) for (r, a), b in zip(even, sides[1])]
    low = total([dot(a, kernel[r, 1]) + dot(b, kernel[r, 2]) for (r, a), (_, b) in zip(even, odd)])
    high = total([dot(a, kernel[r, 0]) + dot(b, kernel[r, 1]) for (r, a), (_, b) in zip(even, odd)])
    west = total([dot(window, kernel[r, 0]) for r, window in left])
    east = total([dot(window, kernel[r, 2]) for r, window in right])
    rows = [
        jnp.concatenate([a + moved_east(c), b + moved_west(d)], axis=1)
        for a, b, c, d in zip(*map(row_parts, (low, high, west, east)))
    ]
    if sides is None:
        return rows
    size = low.shape[0]
    nothing = jnp.zeros((ROWS, HALF), F32)
    ends = jnp.concatenate([west[size:], nothing], axis=1), jnp.concatenate([nothing, east[size:]], axis=1)
    return rows, ends


def step_kernel(
    lists, state_in, factors_in, water, air_in, sea_in, projection_in, coupling_in, out_ref, *scratch
):
    send, scratch = scratch[:N], scratch[N:]
    recv, scratch = scratch[:N], scratch[N:]
    leaving, scratch = scratch[:N], scratch[N:]
    arriving, scratch = scratch[:N], scratch[N:]
    (state, factors, projection, coupling, air, sea, blocks, mask, sums, acc) = scratch[:10]
    (padded_0, padded_1, edges_0, edges_1, corners, rims_0, rims_1, sides, ends, saved, part) = scratch[10:21]
    (labels, marks, places, place_table, orders, order_table) = scratch[21:27]
    (fetch, local_sem, own, sent, landed, mark_sem, over_sent, over_landed, rim_sent, rim_landed) = scratch[27:]

    grp, lat, lon = lax.axis_index("grp"), lax.axis_index("lat"), lax.axis_index("lon")
    me = lat * 16 + lon
    high, x, core = lon // 8, (lon // 2) % 4, lon % 2
    facing = (1 - grp, lat, (lon + 8) % 16)
    west, east = (lon + 15) % 16, (lon + 1) % 16
    north, south = (lat + 3) % 4, (lat + 1) % 4

    def target(k):
        z = (lat + k) % 4
        y = (high + k // 16 + k // 2) % 2
        c = (core + k // 32 + k) % 2
        return z, y * 8 + ((x + k // 4 + k) % 4) * 2 + c

    get_state = pltpu.make_async_copy(state_in, state, fetch.at[0])
    get_factors = pltpu.make_async_copy(factors_in, factors, fetch.at[1])
    get_projection = pltpu.make_async_copy(projection_in, projection, fetch.at[2])
    get_coupling = pltpu.make_async_copy(coupling_in, coupling, fetch.at[3])
    get_air = [pltpu.make_async_copy(air_in.at[layer], air, fetch.at[4 + layer]) for layer in range(2)]
    get_sea = [pltpu.make_async_copy(sea_in.at[layer], sea, fetch.at[4 + layer]) for layer in range(2)]
    get_state.start()
    get_projection.start()
    get_factors.start()
    get_coupling.start()

    def on_air(body):
        pl.when(grp == 0)(body)

    def on_sea(body):
        pl.when(grp == 1)(body)

    on_air(get_air[0].start)
    on_sea(get_sea[0].start)

    barrier = pltpu.get_barrier_semaphore()

    def greet(k, _):
        z, j = target(k)
        pl.semaphore_signal(barrier, inc=1, device_id=(grp, z, j), device_id_type=MESH)
        return 0

    lax.fori_loop(1, TILES, greet, 0)
    pl.semaphore_signal(barrier, inc=1, device_id=facing, device_id_type=MESH)

    place_entries(lists, labels, places)
    tell = pltpu.make_async_copy(places, place_table, local_sem.at[0])
    tell.start()

    def rim_copies(layer, padded, edges, corners, rims):
        pushes = [(padded.at[1], padded.at[17], north, lon), (padded.at[16], padded.at[0], south, lon)]
        for side, j in ((0, west), (1, east)):
            for z, place in ((north, 2), (lat, 1), (south, 0)):
                source = edges if place == 1 else corners
                pushes.append((source.at[side], rims.at[1 - side, place], z, j))
        return [
            pltpu.make_async_remote_copy(
                source,
                goal,
                rim_sent.at[layer, index],
                rim_landed.at[layer, index],
                device_id=(grp, z, j),
                device_id_type=MESH,
            )
            for index, (source, goal, z, j) in enumerate(pushes)
        ]

    get_state.wait()

    @on_air
    def _():
        get_projection.wait()
        air_blocks(state, projection, blocks)

    @on_sea
    def _():
        get_projection.wait()
        sea_blocks(state, water, mask, sums, blocks)

    get_factors.wait()
    tell.wait()

    def payload(slot, start, length):
        factor = factors[place_table[0, slot], start : start + length, :]
        return dot(factor, blocks[place_table[1, slot]]).astype(BF16)

    def own_copy(chunk):
        mine = pl.ds(2 * me, 2)
        return pltpu.make_async_copy(send[chunk].at[mine], recv[chunk].at[mine], own.at[chunk])

    def start_send(chunk, k):
        z, j = target(k)
        pltpu.make_async_remote_copy(
            send[chunk].at[pl.ds(2 * (z * 16 + j), 2)],
            recv[chunk].at[pl.ds(2 * me, 2)],
            sent.at[chunk],
            landed.at[chunk],
            device_id=(grp, z, j),
            device_id_type=MESH,
        ).start()

    def send_payloads(chunk):
        def one(k, _):
            start_send(chunk, k)
            return 0

        lax.fori_loop(1, TILES, one, 0)
        own_copy(chunk).start()

    def first_payloads(k):
        z, j = target(k)
        for i in range(2):
            slot = 2 * (z * 16 + j) + i
            value = payload(slot, 0, 32)
            send[0][slot] = value[0:16]
            send[1][slot] = value[16:32]

    def first_step(k, _):
        first_payloads(k)
        start_send(0, k - 1)
        return 0

    padded_0[1] = activated(state[0])
    padded_0[16] = activated(state[ROWS - 1])
    for side, first in ((0, 0), (1, COLS - 16)):
        group = silu(state[:, first : first + 16, :].astype(F32))
        edges_0[side] = group[:, 15 * side, :].astype(BF16)
    first_rims = rim_copies(0, padded_0, edges_0, edges_0, rims_0)

    pl.semaphore_wait(barrier, TILES)
    def send_label(k, _):
        z, j = target(k)
        pltpu.make_async_remote_copy(
            labels, marks.at[me], mark_sem.at[0], mark_sem.at[1], device_id=(grp, z, j), device_id_type=MESH
        ).start()
        return 0

    lax.fori_loop(1, TILES, send_label, 0)
    own_label = pltpu.make_async_copy(labels, marks.at[me], local_sem.at[1])
    own_label.start()

    for copy in first_rims:
        copy.start()

    first_payloads(0)
    first_payloads(1)
    lax.fori_loop(2, TILES, first_step, 0, unroll=2)
    start_send(0, TILES - 1)
    own_copy(0).start()
    send_payloads(1)

    later = 16 * (CHUNKS[1][0] + 1)

    def later_payloads(slot, _):
        value = payload(slot, later, BLOCK - later)
        for chunk in range(2, N):
            first, count, lane, lanes = CHUNKS[chunk]
            start = 16 * first - later
            send[chunk][slot] = value[start : start + 16 * count, lane : lane + lanes]
        return 0

    lax.fori_loop(0, SLOT_TOTAL, later_payloads, 0, unroll=8)
    send_payloads(2)

    def activate(row, _):
        padded_0[row + 1] = activated(state[row])
        return 0

    lax.fori_loop(1, ROWS - 1, activate, 0, unroll=2)
    for copy in first_rims:
        copy.wait()

    def close_rows(padded):
        @pl.when(lat == 0)
        def _():
            padded[0] = jnp.zeros((COLS, WIDE), BF16)

        @pl.when(lat == 3)
        def _():
            padded[17] = jnp.zeros((COLS, WIDE), BF16)

    def close_sides(rims):
        for side in range(2):
            sides[side, 0:1, :] = rims[side, 0].astype(F32)[15:16] * jnp.where(lat == 0, 0.0, 1.0)
            sides[side, 1:17, :] = rims[side, 1].astype(F32)
            sides[side, 17:18, :] = rims[side, 2].astype(F32)[0:1] * jnp.where(lat == 3, 0.0, 1.0)

    def end_columns():
        @on_air
        def _():
            for side, tap in ((0, 0), (1, 2)):
                ends[side] = total([dot(sides[side, r : r + 16, :].astype(BF16), air[r, tap]) for r in range(3)])

        @on_sea
        def _():
            nothing = jnp.zeros((ROWS, HALF), F32)
            first = total([dot(sides[0, r : r + 16, HALF:].astype(BF16), sea[r, 0]) for r in range(3)])
            final = total([dot(sides[1, r : r + 16, :HALF].astype(BF16), sea[r, 2]) for r in range(3)])
            ends[0] = jnp.concatenate([first, nothing], axis=1)
            ends[1] = jnp.concatenate([nothing, final], axis=1)

    def mixed_rows(mix, kernel):
        def some_rows(step, _):
            windows = [padded_0[pl.ds(4 * step + r, 4)].reshape(4 * COLS, WIDE) for r in range(3)]
            for i, value in enumerate(mix(list(enumerate(windows)), kernel)):
                acc[4 * step + i] = value + state[4 * step + i].astype(F32)
            return 0

        lax.fori_loop(0, 4, some_rows, 0)

    close_rows(padded_0)
    close_sides(rims_0)

    @on_air
    def _():
        get_air[0].wait()
        mixed_rows(mix_air, air)

    @on_sea
    def _():
        get_sea[0].wait()
        mixed_rows(mix_sea, sea)

    end_columns()
    eight = iota((8, 1), 0)

    def add_ends(row, _):
        acc[row, 0:8, :] += jnp.where(eight == 0, ends[0, pl.ds(row, 1), :], 0.0)
        acc[row, COLS - 8 : COLS, :] += jnp.where(eight == 7, ends[1, pl.ds(row, 1), :], 0.0)
        return 0

    lax.fori_loop(0, ROWS, add_ends, 0)
    on_air(get_air[1].start)
    on_sea(get_sea[1].start)
    get_coupling.wait()

    own_label.wait()
    others = pltpu.make_async_remote_copy(
        marks.at[pl.ds(0, TILES - 1)],
        marks.at[pl.ds(0, TILES - 1)],
        mark_sem.at[0],
        mark_sem.at[1],
        device_id=facing,
        device_id_type=MESH,
    )
    others.wait_recv()
    others.wait_send()
    sort_slots(marks, me, orders)
    tell_order = pltpu.make_async_copy(orders, order_table, local_sem.at[2])
    tell_order.start()
    tell_order.wait()

    def crossing(chunk, part):
        half = pl.ds(16 * part, 16)
        return pltpu.make_async_remote_copy(
            leaving[chunk].at[half],
            arriving[chunk].at[half],
            over_sent.at[chunk, part],
            over_landed.at[chunk, part],
            device_id=facing,
            device_id_type=MESH,
        )

    next_sends = [(c + 2,) if 0 < c < N - 2 else () for c in range(N)]

    def sum_and_cross(chunk):
        piece, lanes = PIECES[chunk]
        own_copy(chunk).wait()
        rest = pl.ds(0, SLOT_TOTAL - 2)
        everyone = pltpu.make_async_remote_copy(
            send[chunk].at[rest],
            recv[chunk].at[rest],
            sent.at[chunk],
            landed.at[chunk],
            device_id=facing,
            device_id_type=MESH,
        )
        everyone.wait_recv()
        everyone.wait_send()
        for following in next_sends[chunk]:
            send_payloads(following)

        def accumulate(p, running):
            value = recv[chunk][order_table[0, p]].astype(F32)
            running = jnp.where(order_table[1, p] == 1, 0.0, running) + value
            sums[p, 0:piece, 0:lanes] = running
            return running

        lax.fori_loop(0, SLOT_TOTAL, accumulate, jnp.zeros((piece, lanes), F32), unroll=8)

        def settle(b, _):
            value = jnp.where(order_table[3, b] > 0, sums[order_table[2, b], 0:piece, 0:lanes], 0.0)
            leaving[chunk][b] = value.astype(BF16)
            return 0

        lax.fori_loop(0, 32, settle, 0, unroll=4)
        crossing(chunk, 0).start()
        on_air(crossing(chunk, 1).start)

    def finish_rows(*chunks):
        for chunk in chunks:
            crossing(chunk, 0).wait()
            on_air(crossing(chunk, 1).wait_send)
            on_sea(crossing(chunk, 1).wait_recv)
        first, count = CHUNKS[chunks[0]][:2]
        wanted = [(band, i, 8 * band + first + i) for band in (1, 0) for i in range(count)]

        def given(band, i, blocks_across):
            here = slice(blocks_across * band, blocks_across * (band + 1))
            parts = [arriving[chunk][here, 16 * i : 16 * i + 16, :] for chunk in chunks]
            parts = [part.reshape(16 * blocks_across, part.shape[2]) for part in parts]
            return parts[0] if len(parts) == 1 else jnp.concatenate(parts, axis=1)

        @on_air
        def _():
            for band, i, row in wanted:
                value = (acc[row] + dot(given(band, i, 8), coupling[...])).astype(BF16)
                state[row] = value
                padded_1[row + 1] = activated(value)

        @on_sea
        def _():
            cell, pair = iota((COLS, 2 * COLS), 1), iota((COLS, 2 * COLS), 0)
            for band, i, row in wanted:
                force = given(band, i, 16)
                parts = [dot(ones_where(cell == 2 * pair + side), force) for side in range(2)]
                value = (acc[row] + jnp.concatenate(parts, axis=1)) * mask[row].astype(F32)
                value = value.astype(BF16)
                state[row] = value
                padded_1[row + 1] = activated(value)

    def on_both(body):
        on_air(lambda: body(mix_air, air, lambda row: None))
        on_sea(lambda: body(mix_sea, sea, lambda row: mask[row].astype(F32)))

    def put(row, value, wet):
        value = value + state[row].astype(F32)
        saved[0, row] = value[0:16]
        saved[1, row] = value[COLS - 16 : COLS]
        out_ref[row] = (value if wet is None else value * wet).astype(BF16)

    def window(r, rows):
        return jnp.concatenate([padded_1[row + r] for row in rows], axis=0)

    def last_rows(rows):
        def whole(mix, kernel, wet):
            for row, value in zip(rows, mix([(r, window(r, rows)) for r in range(3)], kernel)):
                put(row, value, wet(row))

        on_both(whole)

    place_of = {3: 0, 4: 1, 5: 2, 11: 3, 12: 4, 13: 5}

    def some_taps(plan, finished=()):
        def taps(mix, kernel, wet):
            found = {}
            for r, rows in plan:
                for row, value in zip(rows, mix([(r, window(r, rows))], kernel)):
                    found.setdefault(row, []).append(value)
            for row, values in found.items():
                value = total(values)
                if plan is not early_taps:
                    value = value + part[place_of[row]]
                if row in finished:
                    put(row, value, wet(row))
                else:
                    part[place_of[row]] = value

        on_both(taps)

    early_taps = ((0, (3, 4, 11, 12)), (1, (3, 5, 11, 13)), (2, (4, 5, 12, 13)))
    late_taps = ((0, (5, 13)), (1, (4, 12)), (2, (3, 11)))

    def take_edges(goal):
        for side, first in ((0, 0), (1, COLS - 16)):
            group = padded_1[1:17, first : first + 16, :].astype(F32)
            goal[side] = group[:, 15 * side, :].astype(BF16)

    last_rims = rim_copies(1, padded_1, edges_1, corners, rims_1)
    early_rims = [last_rims[index] for index in (0, 1, 2, 4, 5, 7)]
    late_rims = [last_rims[index] for index in (3, 6)]

    sum_and_cross(0)
    sum_and_cross(1)
    finish_rows(0)
    sum_and_cross(2)
    finish_rows(1)
    sum_and_cross(3)
    finish_rows(2)
    take_edges(corners)
    for copy in early_rims:
        copy.start()
    sum_and_cross(4)
    finish_rows(3)
    sum_and_cross(5)
    finish_rows(4)
    on_air(get_air[1].wait)
    on_sea(get_sea[1].wait)
    last_rows((1, 7, 8, 9))
    sum_and_cross(6)
    finish_rows(5)
    for copy in early_rims:
        copy.wait()
    close_rows(padded_1)
    last_rows((0, 6, 14, 15))
    sum_and_cross(7)
    sum_and_cross(8)
    finish_rows(6)
    last_rows((2, 10))
    some_taps(early_taps)
    finish_rows(7, 8)
    take_edges(edges_1)
    for copy in late_rims:
        copy.start()
    some_taps(late_taps, (3, 4, 5, 11, 12, 13))
    for copy in late_rims:
        copy.wait()
    close_sides(rims_1)
    end_columns()
    sixteen = iota((16, 1), 0)

    def patch(row, _):
        left = saved[0, row] + jnp.where(sixteen == 0, ends[0, pl.ds(row, 1), :], 0.0)
        right = saved[1, row] + jnp.where(sixteen == 15, ends[1, pl.ds(row, 1), :], 0.0)

        @on_air
        def _():
            out_ref[row, 0:16, :] = left.astype(BF16)
            out_ref[row, COLS - 16 : COLS, :] = right.astype(BF16)

        @on_sea
        def _():
            out_ref[row, 0:16, :] = (left * mask[row, 0:16, :].astype(F32)).astype(BF16)
            out_ref[row, COLS - 16 : COLS, :] = (right * mask[row, COLS - 16 : COLS, :].astype(F32)).astype(BF16)

        return 0

    lax.fori_loop(0, ROWS, patch, 0)


def body(
    state,
    intersection_lists,
    intersection_matrices,
    water_indicator,
    atmosphere_kernels,
    ocean_kernels,
    flux_projection,
    coupling_matrix,
):
    dma = pltpu.SemaphoreType.DMA
    vmem = pl.BlockSpec(memory_space=pltpu.VMEM)
    hbm = pl.BlockSpec(memory_space=pl.ANY)
    tables = pltpu.VMEM((8, SLOT_TOTAL), jnp.int32)
    scalars = pltpu.SMEM((8, SLOT_TOTAL), jnp.int32)
    slots = [pltpu.VMEM((SLOT_TOTAL, *piece), BF16) for piece in PIECES]
    dense = [pltpu.VMEM((32, *piece), BF16) for piece in PIECES]
    result = pl.pallas_call(
        step_kernel,
        out_shape=pltpu.VMEM((ROWS, COLS, WIDE), BF16),
        in_specs=[vmem, hbm, hbm, vmem, hbm, hbm, hbm, hbm],
        out_specs=vmem,
        scratch_shapes=slots
        + slots
        + dense
        + dense
        + [
            pltpu.VMEM((ROWS, COLS, WIDE), BF16),
            pltpu.VMEM((ENTRIES, BLOCK, BLOCK), BF16),
            pltpu.VMEM((WIDE, HALF), BF16),
            pltpu.VMEM((HALF, WIDE), BF16),
            pltpu.VMEM((3, 3, WIDE, WIDE), BF16),
            pltpu.VMEM((3, 3, HALF, HALF), BF16),
            pltpu.VMEM((32, BLOCK, HALF), BF16),
            pltpu.VMEM((ROWS, COLS, WIDE), BF16),
            pltpu.VMEM((SLOT_TOTAL, 32, HALF), F32),
            pltpu.VMEM((ROWS, COLS, WIDE), F32),
            pltpu.VMEM((ROWS + 2, COLS, WIDE), BF16),
            pltpu.VMEM((ROWS + 2, COLS, WIDE), BF16),
            pltpu.VMEM((2, 16, WIDE), BF16),
            pltpu.VMEM((2, 16, WIDE), BF16),
            pltpu.VMEM((2, 16, WIDE), BF16),
            pltpu.VMEM((2, 3, 16, WIDE), BF16),
            pltpu.VMEM((2, 3, 16, WIDE), BF16),
            pltpu.VMEM((2, 24, WIDE), F32),
            pltpu.VMEM((2, 16, WIDE), F32),
            pltpu.VMEM((2, ROWS, 16, WIDE), F32),
            pltpu.VMEM((6, COLS, WIDE), F32),
            pltpu.VMEM((1, SLOT_TOTAL), jnp.int32),
            pltpu.VMEM((TILES, 1, SLOT_TOTAL), jnp.int32),
            tables,
            scalars,
            tables,
            scalars,
            dma((6,)),
            dma((3,)),
            dma((N,)),
            dma((N,)),
            dma((N,)),
            dma((2,)),
            dma((N, 2)),
            dma((N, 2)),
            dma((2, 8)),
            dma((2, 8)),
        ],
        compiler_params=pltpu.CompilerParams(
            collective_id=0, has_side_effects=True, vmem_limit_bytes=58 << 20
        ),
    )(
        intersection_lists.reshape(3, 1, ENTRIES),
        state[0],
        intersection_matrices.reshape(ENTRIES, BLOCK, BLOCK),
        water_indicator,
        atmosphere_kernels,
        ocean_kernels,
        flux_projection,
        coupling_matrix,
    )
    return result[None]


def solution(mesh):
    placed = (
        P("grp", "lat", "lon", None),
        P("grp", "lat", "lon", None, None),
        P("grp", "lat", "lon", None, None, None),
        P("lat", "lon"),
        P(),
        P(),
        P(),
        P(),
    )
    return jax.shard_map(
        body, mesh=mesh, in_specs=placed, out_specs=P("grp", "lat", "lon", None), check_vma=False
    )
```
